128 devices in a mesh: gx: 16 (over y, z_lo, core), gy: 8 (over x, z_hi).
Axes of the slice: x: 4, y: 4, z: 4 (z_hi: 2, z_lo: 2; z = z_hi * 2 + z_lo), core: 2. Of those that a mesh axis runs over, the one named last changes fastest.
Arguments:
- fields: bfloat16 [8, 256, 128, 128], P(None, ('gx', 'gy')), may hold values from -6 to 6
- w_lift: bfloat16 [3, 3, 3, 8, 64], replicated, may hold values from -0.4375 to 0.4375
- b_lift: float32 [64], replicated, may hold values from -3 to 3
- down_weight: bfloat16 [4, 4, 4, 64, 64], replicated, may hold values from -0.09375 to 0.09375
- b_down: float32 [64], replicated, may hold values from -3 to 3
- perf_well: int32 [128, 256], P(('gx', 'gy')), may hold values from -1 to 2047, as said below
- perf_cell: int32 [128, 256], P(('gx', 'gy')), may hold values from 0 to 4095, as said below
- perf_weight: float32 [128, 256], P(('gx', 'gy')), may hold values from 0.25 to 2
- well_slot: int32 [2048], replicated, may hold values from 0 to 2047, each once
- well_grad: bfloat16 [2048, 64], P(('gx', 'gy')), may hold values from -24 to 24
- field_grad: bfloat16 [64, 64, 64, 128], P(None, 'gx', 'gy'), may hold values from -6 to 6
Outputs:
- coarse: bfloat16 [64, 64, 64, 128], P(None, 'gx', 'gy')
- well_feat: float32 [2048, 64], P(('gx', 'gy'))
- down_grad: float32 [4, 4, 4, 64, 64], replicated
The draws below stay inside these ranges and needn't reach their ends.
Inputs may be any that keep to these rules, and one draw needn't show every extreme that they name: `perf_well`: entry -1 marks an empty slot. Every well appears in exactly 8 slots of one row, the perforations of one vertical well at consecutive depths. Some row has all 256 slots used in every draw. `perf_cell`: local index (x * 8 + y) * 128 + z of the perforated cell in the row's tile of 4 x 8 x 128 coarse cells; 0 in empty slots. `well_slot`: A permutation; row r is held by the device of index r // 16 along gx+gy.
All inputs are finite; a program needn't handle non-finite values.
Results may differ from the reference program's by a relative error of at most 0.0045.
Values may be sent and summed in bfloat16 or wider, within the bound.
No kernel may reach another device: no remote copies, remote signals or barrier semaphores. Data moves between devices by JAX's collectives and lax.ppermute only.
A program may use at most 128 MiB of HBM per device.

```python
import math
import jax
import jax.numpy as jnp
from jax import lax

CIN = 8
C = 64
NZ = 256
WELL_DEV = 16
PERF = 8
PERF_DEV = 256
WELLS = 2048
NX = 128
NY = 128
HX = 4
HY = 8
NZH = 128
NXH = 64
NYH = 64
N_GY = 8
DEVICES = 128


def perforation_lists(key):
    base_key = jax.random.fold_in(key, 1234)
    key_order, key_wells, key_col, key_row, key_top = jax.random.split(base_key, 5)
    quarter = WELL_DEV // 4
    pattern = jnp.tile(jnp.array([8, 4, 3, 1], jnp.int32) * quarter, DEVICES // 4)
    counts = pattern[jax.random.permutation(key_order, DEVICES)]
    offsets = jnp.cumsum(counts) - counts
    well_order = jax.random.permutation(key_wells, WELLS).astype(jnp.int32)
    max_wells = PERF_DEV // PERF
    local_well = jnp.arange(PERF_DEV, dtype=jnp.int32) // PERF
    layer_index = jnp.arange(PERF_DEV, dtype=jnp.int32) % PERF
    is_used = local_well[None, :] < counts[:, None]
    list_index = jnp.clip(offsets[:, None] + local_well[None, :], 0, WELLS - 1)
    well_ids = jnp.where(is_used, well_order[list_index], -1).astype(jnp.int32)
    column_x = jax.random.randint(key_col, (DEVICES, max_wells), 0, HX).astype(jnp.int32)
    column_y = jax.random.randint(key_row, (DEVICES, max_wells), 0, HY).astype(jnp.int32)
    uppermost_layer = jax.random.randint(key_top, (DEVICES, max_wells), 0, NZH - PERF + 1).astype(jnp.int32)
    column_x = column_x.at[:, 0].set(HX - 1)
    column_y = column_y.at[:, 0].set(HY - 1)
    uppermost_layer = uppermost_layer.at[:, 0].set(NZH - PERF)
    cell_ids = (column_x[:, local_well] * HY + column_y[:, local_well]) * NZH + uppermost_layer[:, local_well] + layer_index[None, :]
    cell_ids = jnp.where(is_used, cell_ids, 0).astype(jnp.int32)
    return (well_ids, cell_ids)


def draw_perf_well(key, part):
    return perforation_lists(key)[0]


def draw_perf_cell(key, part):
    return perforation_lists(key)[1]


def block_levels(rng, dims, cuts, low, high):
    loudness, own = 1.0, jax.random.fold_in(rng, 6)
    for axis_at, shards_of in cuts:
        steps = jnp.exp(jax.random.uniform(jax.random.fold_in(own, axis_at), (shards_of,), jnp.float32, low / len(cuts), high / len(cuts)))
        loudness = loudness * jnp.repeat(steps, dims[axis_at] // shards_of).reshape([-1 if axis == axis_at else 1 for axis in range(len(dims))])
    return loudness


def gaussian(key, dims, width, limit, cuts=(), kind=jnp.bfloat16):
    result = jax.random.normal(key, dims, jnp.float32) * width
    if len(cuts) > 0:
        result = block_levels(key, dims, cuts, -0.22, 0.18) * result
    return jnp.clip(result, min=-limit, max=limit).astype(kind)


def setup_inputs(seed: int = 0) -> dict:
    seeds = jax.random.split(jax.random.key(seed), 12)
    fields = gaussian(seeds[0], (CIN, NZ, NX, NY), 1.0, 6.0, ((1, 128),))
    w_lift = gaussian(seeds[1], (3, 3, 3, CIN, C), (27 * CIN) ** -0.5, 0.4375)
    b_lift = gaussian(seeds[2], (C,), 0.5, 3.0, (), jnp.float32)
    down_weight = gaussian(seeds[3], (4, 4, 4, C, C), (64 * C) ** -0.5, 0.09375)
    b_down = gaussian(seeds[4], (C,), 0.5, 3.0, (), jnp.float32)
    perf_well = draw_perf_well(jax.random.fold_in(seeds[11], 71), 0)
    perf_cell = draw_perf_cell(jax.random.fold_in(seeds[11], 71), 0)
    perf_weight = jnp.clip(jnp.exp(math.log(2.0) - 2.0794415 * jax.random.uniform(seeds[7], (DEVICES, PERF_DEV), jnp.float32) ** block_levels(seeds[7], (DEVICES, PERF_DEV), ((0, 128),), -0.2, 0.2)), 0.25, 2.0)
    well_slot = jax.random.permutation(seeds[8], WELLS).astype(jnp.int32)
    well_grad = gaussian(seeds[9], (WELLS, C), 4.0, 24.0, ((0, 128),))
    field_grad = gaussian(seeds[10], (C, NXH, NYH, NZH), 1.0, 6.0, ((1, 16), (2, 8)))
    return {"fields": fields, "w_lift": w_lift, "b_lift": b_lift, "down_weight": down_weight, "b_down": b_down, "perf_well": perf_well, "perf_cell": perf_cell, "perf_weight": perf_weight, "well_slot": well_slot, "well_grad": well_grad, "field_grad": field_grad}


def reference(fields, w_lift, b_lift, down_weight, b_down, perf_well, perf_cell, perf_weight, well_slot, well_grad, field_grad):
    layout_spec = ('NCDHW', 'DHWIO', 'NCDHW')
    highest = lax.Precision.HIGHEST
    volume = jnp.transpose(fields, (0, 2, 3, 1)).astype(jnp.float32)[None]
    lifted = lax.conv_general_dilated(volume, w_lift.astype(jnp.float32), (1, 1, 1), ((1, 1), (1, 1), (1, 1)), dimension_numbers=layout_spec, precision=highest)
    hidden = jax.nn.gelu(lifted[0] + b_lift[:, None, None, None]).astype(jnp.bfloat16)
    hidden_wide = hidden.astype(jnp.float32)[None]

    def reduce_resolution(kernel_taps):
        return lax.conv_general_dilated(hidden_wide, kernel_taps, (2, 2, 2), ((1, 1), (1, 1), (1, 1)), dimension_numbers=layout_spec, precision=highest)
    stepped_convolve, backward_map = jax.vjp(reduce_resolution, down_weight.astype(jnp.float32))
    coarse = (stepped_convolve[0] + b_down[:, None, None, None]).astype(jnp.bfloat16)
    device_ids = jnp.arange(DEVICES, dtype=jnp.int32)[:, None]
    tile_col = device_ids // N_GY
    tile_row = device_ids % N_GY
    coord_u = tile_col * HX + perf_cell // (HY * NZH)
    coord_v = tile_row * HY + perf_cell // NZH % HY
    coord_w = perf_cell % NZH
    is_used = perf_well >= 0
    slot = jnp.where(is_used, well_slot[jnp.clip(perf_well, 0, WELLS - 1)], WELLS).astype(jnp.int32)
    values = coarse[:, coord_u, coord_v, coord_w].astype(jnp.float32) * perf_weight[None]
    well_feat = jnp.zeros((WELLS, C), jnp.float32).at[slot.reshape(-1)].add(values.reshape(C, -1).T, mode='drop')
    pulled = well_grad[jnp.clip(slot, 0, WELLS - 1)].astype(jnp.float32) * perf_weight[..., None]
    pulled = jnp.where(is_used[..., None], pulled, jnp.float32(0.0))
    cotangent = field_grad.astype(jnp.float32).at[:, coord_u, coord_v, coord_w].add(jnp.moveaxis(pulled, 2, 0))
    cotangent = cotangent.astype(jnp.bfloat16)
    grad_scale = 1.0 / math.sqrt(NXH * NYH * NZH)
    down_grad = backward_map(cotangent.astype(jnp.float32)[None])[0] * grad_scale
    return (coarse, well_feat, down_grad)
```

```python
import math

import jax
import jax.numpy as jnp
from jax import lax
from jax.experimental import pallas as pl
from jax.experimental.pallas import tpu as pltpu
from jax.sharding import PartitionSpec as P

BF = jnp.bfloat16
F32 = jnp.float32
I32 = jnp.int32
AXES = ("gx", "gy")
INTERPRET = False
ROOT_2_PI = math.sqrt(2.0 / math.pi)


def dot_nn(a, b):
    return lax.dot_general(a, b, (((1,), (0,)), ((), ())), preferred_element_type=F32)


def dot_nt(a, b):
    return lax.dot_general(a, b, (((1,), (1,)), ((), ())), preferred_element_type=F32)


def iota(shape, dim):
    return lax.broadcasted_iota(I32, shape, dim)


def ones_where(mask):
    return jnp.where(mask, 1.0, 0.0).astype(BF)


def split(x):
    high = x.astype(BF)
    return high, (x - high.astype(F32)).astype(BF)


def pack_kernel(fields_ref, wells_ref, out_ref):
    lane = iota((1, 1024), 1)
    within = lane & 127
    which = (within * 205) >> 12
    y = (lane >> 7) * 16 - 2 + within - 20 * which
    target = jnp.where((which < 6) & (y >= 0) & (y < 128), which * 128 + y, -1)
    spread = ones_where(iota((768, 1024), 0) == target)
    row, col = iota((256, 144), 0), iota((256, 144), 1)
    xx = row & 15
    windows = ones_where(
        ((xx < 12) & (col < 128) & (col == (row >> 4) * 8 - 2 + xx))
        | ((xx >= 12) & (col - 128 == xx))
    )
    empty = jnp.zeros((128, 128), BF)
    for group in range(3):
        planes = [
            fields_ref[6 * group + j] if 6 * group + j < 16 else empty for j in range(6)
        ]
        lined = dot_nn(jnp.concatenate(planes, axis=1), spread).astype(BF)
        if group < 2:
            piece = wells_ref[:, 128 * group : 128 * group + 128]
        else:
            piece = jnp.zeros((16, 128), BF)
        lined = jnp.concatenate([lined, jnp.concatenate([piece] * 8, axis=1)], axis=0)
        blocks = dot_nn(windows, lined).astype(BF).reshape(16, 16, 1024)
        for b in range(8):
            out_ref[:, b, :, 128 * group : 128 * group + 128] = blocks[
                :, :, 128 * b : 128 * b + 128
            ]


def prep_kernel(
    well_ref,
    cell_ref,
    table_ref,
    lift_ref,
    down_ref,
    field_ref,
    cells_ref,
    rows_ref,
    quarter_ref,
    owner_ref,
    lanes_ref,
    big_ref,
    taps_ref,
    grad_ref,
):
    well = well_ref[...]
    used = well >= 0
    cells_ref[...] = ones_where(iota((4096, 256), 0) == jnp.where(used, cell_ref[...], -1))
    matches = ones_where(iota((2048, 256), 0) == well)
    table = table_ref[...]
    row = iota((8, 2048), 0)
    digits = jnp.where(row == 0, table >> 4, jnp.where(row == 1, table & 15, 0))
    found = dot_nn(digits.astype(F32).astype(BF), matches)
    slot = jnp.where(used, (found[0:1] * 16.0 + found[1:2]).astype(I32), -1)
    for half in range(2):
        place = jnp.where(
            used & (((slot >> 3) & 1) == half), (slot >> 4) * 8 + (slot & 7), -1
        )
        owner_ref[:, 256 * half : 256 * half + 256] = ones_where(iota((1024, 256), 0) == place)
    column = jnp.transpose(jnp.broadcast_to(slot, (128, 256)).astype(F32))[:, 0:1].astype(I32)
    place = jnp.where(column >= 0, ((column >> 2) & 3) * 128 + (column >> 4), -1)
    rows_ref[...] = ones_where(iota((256, 512), 1) == place)
    quarter_ref[...] = jnp.where((iota((256, 256), 1) >> 6) == (column & 3), 1.0, 0.0)

    lane = iota((1, 1152), 1)
    plane = lane & 15
    group = (plane * 43) >> 8
    target = (
        ((lane >> 4) & 1) * 384
        + group * 128
        + (plane - 6 * group) * 20
        + 2 * (lane >> 7)
        + ((lane >> 5) & 3)
    )
    lanes_ref[...] = ones_where(iota((768, 1152), 0) == target)

    row = iota((256, 1), 0)
    x = 2 * (row >> 7) + ((row >> 4) & 1)
    y = (row >> 5) & 3
    channel = (row >> 1) & 7
    col = iota((256, 256), 1)
    for ds in range(2):
        z = 2 * ds + (row & 1)
        for px in range(2):
            for py in range(2):
                parts = []
                for pz in range(2):
                    i, j, k = x - px, y - py, z - pz
                    good = (i >= 0) & (i < 3) & (j >= 0) & (j < 3) & (k >= 0) & (k < 3)
                    tap = jnp.where(good, ((i * 3 + j) * 3 + k) * 8 + channel, -1)
                    parts.append(ones_where(col == tap))
                block = dot_nn(jnp.concatenate(parts, axis=1), lift_ref[...])
                at = ds * 512 + (px * 2 + py) * 128
                big_ref[:, at : at + 128] = block.astype(BF)

    eye = ones_where(iota((64, 64), 0) == iota((64, 64), 1))
    turned = dot_nt(eye, down_ref[...]).astype(BF)
    for a in range(2):
        for b in range(2):
            for d in range(2):
                for p in range(4):
                    at = ((2 * a + p // 2) * 4 + 2 * b + p % 2) * 256 + d * 128
                    taps_ref[2 * a + b, 64 * d : 64 * d + 64, 128 * p : 128 * p + 128] = turned[
                        :, at : at + 128
                    ]

    row, col = iota((256, 256), 0), iota((256, 256), 1)
    turn = ones_where(col == (row & 7) * 32 + (row >> 3))
    for g in range(8):
        part = dot_nn(turn, field_ref[8 * g : 8 * g + 8].reshape(256, 128))
        for uv in range(32):
            grad_ref[8 * g : 8 * g + 8, 128 * uv : 128 * uv + 128] = part[
                8 * uv : 8 * uv + 8
            ]


def lift_kernel(
    tile_ref,
    arrived_ref,
    weight_ref,
    bias_ref,
    cells_ref,
    rows_ref,
    quarter_ref,
    lanes_ref,
    big_ref,
    grad_ref,
    send_ref,
    pairs_ref,
    last_ref,
    sorted_ref,
    wells_ref,
    window_ref,
    raw_ref,
    tail_ref,
    cot_ref,
    sum_ref,
):
    a, b = tile_ref[0], tile_ref[1]

    row, col = iota((256, 256), 0), iota((256, 256), 1)
    place = row >> 4
    x = jnp.where(place < 6, 2 * place, jnp.where(place < 12, 2 * place - 11, place))
    turn = ones_where(col == (row & 15) * 16 + x)

    def sort(g, carry):
        block = arrived_ref[pl.ds(16 * g, 16)].reshape(256, 384)
        part = dot_nn(turn, block).astype(BF)
        for xp in range(2):
            for x2 in range(6):
                at = 16 * (6 * xp + x2)
                sorted_ref[
                    pl.ds(pl.multiple_of(128 * x2 + 16 * g, 16), 16), 384 * xp : 384 * xp + 384
                ] = part[at : at + 16]
        for t in range(4):
            wells_ref[pl.ds(pl.multiple_of(128 * t + 16 * g, 16), 16), :] = part[
                192 + 16 * t : 208 + 16 * t, 0:256
            ]
        return carry

    lax.fori_loop(0, 8, sort, 0)

    def lanes(x2, carry):
        at = pl.multiple_of(128 * x2, 128)
        part = dot_nn(sorted_ref[pl.ds(at, 128), :], lanes_ref[...]).astype(BF)
        for v in range(9):
            window_ref[v, pl.ds(at, 128), :] = part[:, 128 * v : 128 * v + 128]
        return carry

    lax.fori_loop(0, 6, lanes, 0)

    lane = iota((64, 256), 1)
    fold = ones_where((lane & 63) == iota((64, 256), 0))
    pulled = (dot_nn(rows_ref[...], wells_ref[...]) * quarter_ref[...]).astype(BF)
    spread = dot_nt(fold, pulled) * weight_ref[...]
    added = dot_nt(jnp.concatenate(split(spread), axis=0), cells_ref[...])
    grown = (grad_ref[...] + added[0:64] + added[64:128]).astype(BF)
    cot_ref[0:64, :] = grown
    lane = iota((64, 128), 1)
    ends = jnp.zeros((64, 128), F32)
    for uv in range(32):
        piece = grown[:, 128 * uv : 128 * uv + 128].astype(F32)
        moved = pltpu.roll(piece, 1, 1)
        cot_ref[64:128, 128 * uv : 128 * uv + 128] = jnp.where(lane == 0, 0.0, moved).astype(BF)
        at = (uv // 8) * 9 + uv % 8
        ends = jnp.where(lane == at, pltpu.roll(piece, at + 1, 1), ends)

    lane = iota((1, 512), 1)
    px, py, pz = lane >> 8, (lane >> 7) & 1, (lane >> 6) & 1
    bias = bias_ref[...]

    def active(v):
        return 0.5 * v * (1.0 + jnp.tanh(ROOT_2_PI * (v + 0.044715 * (v * v * v))))

    def inside(u, v):
        left = jnp.where((a == 0) & (u == 0), 0.0, 1.0)
        right = jnp.where((a == 15) & (u == 4), 0.0, 1.0)
        low = jnp.where((b == 0) & (v == 0), 0.0, 1.0)
        high = jnp.where((b == 7) & (v == 8), 0.0, 1.0)
        return jnp.where(px == 0, left, right) * jnp.where(py == 0, low, high)

    tail_ref[...] = jnp.zeros((128, 512), F32)
    first = iota((128, 512), 0) == 0
    start = jnp.where(first & (pz == 0), 0.0, 1.0)

    def strip(v, carry):
        window = window_ref[v]
        both = jnp.concatenate([window[0:640], window[128:768]], axis=1)
        raw_ref[...] = dot_nn(both, big_ref[...])

        def cell(u, inner):
            at = pl.multiple_of(128 * u, 128)
            before = raw_ref[pl.ds(at, 128), 0:512]
            after = raw_ref[pl.ds(at, 128), 512:1024]
            keep = inside(u, v)
            ending = active(before[127:128] + bias) * keep * jnp.where(pz == 0, 1.0, 0.0)
            tail_ref[pl.ds(u * 9 + v, 1), :] = ending
            moved = jnp.where(first, 0.0, pltpu.roll(before, 1, 0))
            value = active(moved + after + bias) * (keep * start)
            pairs_ref[u, v] = value.astype(BF)
            return inner

        return lax.fori_loop(0, 5, cell, carry)

    lax.fori_loop(0, 9, strip, 0)
    last = tail_ref[...].astype(BF)
    last_ref[...] = last

    sum_ref[...] = jnp.zeros((512, 512), F32)
    for i in range(2):
        for j in range(2):
            shift = 9 * i + j
            edge = (pltpu.roll(ends, shift, 1) if shift else ends).astype(BF)
            at = 128 * (2 * i + j) + 64
            sum_ref[at : at + 64, :] = dot_nn(edge, last)

    def gather(u, carry):
        cot = cot_ref[:, pl.ds(pl.multiple_of(1024 * u, 1024), 1024)]
        for i in range(2):
            for j in range(2):
                group = pairs_ref[u + i, j : j + 8].reshape(1024, 512)
                at = 128 * (2 * i + j)
                sum_ref[at : at + 128, :] += dot_nn(cot, group)
        return carry

    lax.fori_loop(0, 4, gather, 0)
    for r in range(32):
        for j in range(4):
            send_ref[4 * r + j] = sum_ref[16 * r : 16 * r + 16, 128 * j : 128 * j + 128].astype(BF)


def coarse_kernel(
    pairs_ref,
    last_ref,
    taps_ref,
    bias_ref,
    weight_ref,
    cells_ref,
    owner_ref,
    coarse_ref,
    feat_ref,
    wide_ref,
):
    lane = iota((64, 128), 1)
    edge = jnp.zeros((64, 128), F32)
    for i in range(2):
        for j in range(2):
            part = dot_nt(taps_ref[2 * i + j, 64:128, :], last_ref[...])
            shift = (128 - 9 * i - j) % 128
            edge = edge + (pltpu.roll(part, shift, 1) if shift else part)
    bias = bias_ref[...]

    def layer(u, carry):
        total = None
        for i in range(2):
            for j in range(2):
                group = pairs_ref[u + i, j : j + 8].reshape(1024, 512)
                part = dot_nt(taps_ref[2 * i + j], group)
                total = part if total is None else total + part
        for v in range(8):
            near = total[0:64, 128 * v : 128 * v + 128]
            deep = pltpu.roll(total[64:128, 128 * v : 128 * v + 128], 127, 1)
            end = pltpu.roll(edge, 127 - (9 * u + v), 1)
            value = near + jnp.where(lane == 127, end, deep) + bias
            at = pl.multiple_of(1024 * u + 128 * v, 128)
            wide_ref[:, pl.ds(at, 128)] = value
        return carry

    lax.fori_loop(0, 4, layer, 0)

    picked = dot_nn(wide_ref[...].astype(BF), cells_ref[...]) * weight_ref[...]
    feat = jnp.zeros((1024, 128), F32)
    none = jnp.zeros((64, 256), BF)
    for part in split(picked):
        twice = jnp.concatenate(
            [jnp.concatenate([part, none], axis=1), jnp.concatenate([none, part], axis=1)], axis=0
        )
        feat = feat + dot_nt(owner_ref[...], twice)
    feat_ref[...] = feat.astype(BF).reshape(128, 8, 128)

    row, col = iota((256, 256), 0), iota((256, 256), 1)
    turn = ones_where(col == (row & 31) * 8 + (row >> 5))
    for g in range(8):
        tall = jnp.concatenate(
            [wide_ref[8 * g : 8 * g + 8, 128 * uv : 128 * uv + 128] for uv in range(32)], axis=0
        )
        part = dot_nn(turn, tall.astype(BF)).astype(BF)
        coarse_ref[8 * g : 8 * g + 8] = part.reshape(8, 32, 128)


def sum_kernel(scale, parts_ref, feat_ref, out_ref):
    total = jnp.sum(parts_ref[...].astype(F32), axis=0) * scale
    out_ref[:, 0:16, :] = jnp.broadcast_to(total.astype(BF)[None], (128, 16, 128))
    out_ref[:, 16:24, :] = feat_ref[...]


def finish_kernel(arrived_ref, grad_ref, feat_ref):
    eye = ones_where(iota((128, 128), 0) == iota((128, 128), 1))
    for a in range(2):
        for b in range(2):
            for d in range(2):
                base = 4 * (4 * a + 2 * b + d)
                for p in range(4):
                    block = jnp.concatenate(
                        [arrived_ref[4 * (base + t) + p, 0:16, :] for t in range(4)], axis=0
                    )
                    tap = ((2 * a + p // 2) * 4 + 2 * b + p % 2) * 4 + 2 * d
                    grad_ref[64 * tap : 64 * tap + 128, :] = dot_nt(eye, block)
    feat = jnp.sum(arrived_ref[:, 16:24, :].astype(F32), axis=0)
    feat_ref[0:8, :] = feat[:, 0:64]
    feat_ref[8:16, :] = pltpu.roll(feat, 64, 1)[:, 0:64]


def call(kernel, outs, scratch=(), scalars=0, cost=0):
    extra = {}
    if scalars:
        extra["in_specs"] = [pl.BlockSpec(memory_space=pltpu.SMEM)] + [
            pl.BlockSpec(memory_space=pltpu.VMEM)
        ] * scalars
    return pl.pallas_call(
        kernel,
        out_shape=[jax.ShapeDtypeStruct(shape, dtype) for shape, dtype in outs],
        scratch_shapes=[pltpu.VMEM(shape, dtype) for shape, dtype in scratch],
        compiler_params=pltpu.CompilerParams(vmem_limit_bytes=56 << 20),
        cost_estimate=pl.CostEstimate(flops=cost, bytes_accessed=1 << 20, transcendentals=0),
        interpret=INTERPRET,
        **extra,
    )


def pack(fields, well_grad):
    wells = jnp.pad(well_grad.reshape(4, 256), ((12, 0), (0, 0)))
    return call(pack_kernel, [((16, 8, 16, 384), BF)], cost=1 << 31)(
        fields.reshape(16, 128, 128), wells
    )[0].reshape(128, 16, 384)


def prepare(perf_well, perf_cell, well_slot, w_lift, down_weight, field_grad):
    flat = jnp.pad(w_lift.reshape(216, 64), ((0, 40), (0, 0)))
    none = jnp.zeros_like(flat)
    lift = jnp.concatenate(
        [jnp.concatenate([flat, none], axis=1), jnp.concatenate([none, flat], axis=1)], axis=0
    )
    outs = [
        ((4096, 256), BF),
        ((256, 512), BF),
        ((256, 256), F32),
        ((1024, 512), BF),
        ((768, 1152), BF),
        ((256, 1024), BF),
        ((4, 128, 512), BF),
        ((64, 4096), F32),
    ]
    return call(prep_kernel, outs, cost=1 << 32)(
        perf_well,
        perf_cell,
        well_slot.reshape(1, 2048),
        lift,
        down_weight.reshape(4096, 64),
        field_grad.reshape(64, 32, 128),
    )


def lift(tile, arrived, perf_weight, b_lift, cells, rows, quarter, lanes, big, grad):
    outs = [((128, 16, 128), BF), ((5, 9, 128, 512), BF), ((128, 512), BF)]
    scratch = [
        ((768, 768), BF),
        ((512, 256), BF),
        ((9, 768, 128), BF),
        ((640, 1024), F32),
        ((128, 512), F32),
        ((128, 4096), BF),
        ((512, 512), F32),
    ]
    return call(lift_kernel, outs, scratch, scalars=9, cost=1 << 33)(
        tile,
        arrived,
        perf_weight,
        jnp.tile(b_lift, 8)[None, :],
        cells,
        rows,
        quarter,
        lanes,
        big,
        grad,
    )


def coarsen(pairs, last, taps, b_down, perf_weight, cells, owner):
    outs = [((64, 32, 128), BF), ((128, 8, 128), BF)]
    return call(coarse_kernel, outs, [((64, 4096), F32)], cost=1 << 33)(
        pairs, last, taps, b_down[:, None], perf_weight, cells, owner
    )


def exchange(blocks):
    return lax.all_to_all(blocks, AXES, split_axis=0, concat_axis=0, tiled=True)


def body(
    fields,
    w_lift,
    b_lift,
    down_weight,
    b_down,
    perf_well,
    perf_cell,
    perf_weight,
    well_slot,
    well_grad,
    field_grad,
):
    scale = 1.0 / math.sqrt(64 * 64 * 128)
    tile = jnp.stack([lax.axis_index("gx"), lax.axis_index("gy")]).astype(I32)
    arrived = exchange(pack(fields, well_grad))
    cells, rows, quarter, owner, lanes, big, taps, grad = prepare(
        perf_well, perf_cell, well_slot, w_lift, down_weight, field_grad
    )
    parts, pairs, last = lift(
        tile, arrived, perf_weight, b_lift, cells, rows, quarter, lanes, big, grad
    )
    parts = exchange(parts)
    coarse, feat = coarsen(pairs, last, taps, b_down, perf_weight, cells, owner)
    shared = call(
        lambda *refs: sum_kernel(scale, *refs), [((128, 24, 128), BF)], cost=1 << 20
    )(parts, feat)[0]
    shared = exchange(shared)
    down_grad, well_feat = call(
        finish_kernel, [((4096, 64), F32), ((16, 64), F32)], cost=1 << 28
    )(shared)
    return (
        coarse.reshape(64, 4, 8, 128),
        well_feat,
        down_grad.reshape(4, 4, 4, 64, 64),
    )


def solution(mesh):
    placed = (
        P(None, AXES, None, None),
        P(),
        P(),
        P(),
        P(),
        P(AXES, None),
        P(AXES, None),
        P(AXES, None),
        P(),
        P(AXES, None),
        P(None, "gx", "gy", None),
    )
    return jax.shard_map(
        body,
        mesh=mesh,
        in_specs=placed,
        out_specs=(P(None, "gx", "gy", None), P(AXES, None), P()),
        check_vma=False,
    )
```

```python
import math

import jax
import jax.numpy as jnp
from jax import lax
from jax.experimental import pallas as pl
from jax.experimental.pallas import tpu as pltpu
from jax.sharding import PartitionSpec as P

BF = jnp.bfloat16
F32 = jnp.float32
I32 = jnp.int32
AXES = ("gx", "gy")
INTERPRET = False
ROOT_2_PI = math.sqrt(2.0 / math.pi)


def dot_nn(a, b):
    return lax.dot_general(a, b, (((1,), (0,)), ((), ())), preferred_element_type=F32)


def dot_nt(a, b):
    return lax.dot_general(a, b, (((1,), (1,)), ((), ())), preferred_element_type=F32)


def iota(shape, dim):
    return lax.broadcasted_iota(I32, shape, dim)


def ones_where(mask):
    return jnp.where(mask, 1.0, 0.0).astype(BF)


def split(x):
    high = x.astype(BF)
    return high, (x - high.astype(F32)).astype(BF)


def pack_kernel(fields_ref, wells_ref, out_ref):
    row = iota((320, 1), 0)
    b = (row * 205) >> 13
    rho = row - 40 * b
    group = jnp.where(rho >= 20, 1, 0)
    t = rho - 20 * group
    y = 16 * b - 2 + t
    target = jnp.where((y >= 0) & (y < 128), group * 128 + y, -1)
    windows = ones_where(iota((320, 256), 1) == target)
    empty = jnp.zeros((128, 128), BF)

    def plane(j):
        return jnp.concatenate([fields_ref[j], fields_ref[10 + j] if j < 6 else empty], axis=1)

    lined = jnp.concatenate(
        [
            dot_nt(windows, jnp.concatenate([plane(2 * j), plane(2 * j + 1)], axis=0)).astype(BF)
            for j in range(5)
        ],
        axis=1,
    )
    channel, lane = iota((64, 128), 0), iota((64, 128), 1)
    wells = wells_ref[...]
    placed = jnp.concatenate(
        [
            dot_nn(wells, ones_where((channel >= 56) & (lane == channel + 64))),
            dot_nn(wells, ones_where((channel < 56) & (lane == channel + 72))),
        ],
        axis=0,
    ).astype(BF)
    target = jnp.where(t < 16, 16 * group + t, -1)
    extra = dot_nn(ones_where(iota((320, 32), 1) == target), placed)
    extra = jnp.concatenate([extra] * 4, axis=1)
    for part in range(4):
        lane = iota((1, 512), 1)
        within = lane & 127
        which = (within * 171) >> 11
        x = (lane >> 7) * 8 + 32 * part - 2 + within - 12 * which
        target = jnp.where((which < 10) & (x >= 0) & (x < 128), which * 128 + x, -1)
        spread = ones_where(iota((1280, 512), 0) == target)
        blocks = (dot_nn(lined, spread) + extra).astype(BF)
        for a in range(4):
            out_ref[4 * part + a] = blocks[:, 128 * a : 128 * a + 128].reshape(8, 40, 128)


def prep_kernel(
    well_ref,
    cell_ref,
    table_ref,
    lift_ref,
    down_ref,
    field_ref,
    cells_ref,
    rows_ref,
    half_ref,
    owner_ref,
    lanes_ref,
    big_ref,
    taps_ref,
    grad_ref,
):
    well = well_ref[...]
    used = well >= 0
    cells_ref[...] = ones_where(iota((4096, 256), 0) == jnp.where(used, cell_ref[...], -1))
    matches = ones_where(iota((2048, 256), 0) == well)
    table = table_ref[...]
    row = iota((8, 2048), 0)
    digits = jnp.where(row == 0, table >> 4, jnp.where(row == 1, table & 15, 0))
    found = dot_nn(digits.astype(F32).astype(BF), matches)
    slot = jnp.where(used, (found[0:1] * 16.0 + found[1:2]).astype(I32), -1)
    for half in range(2):
        place = jnp.where(
            used & (((slot >> 3) & 1) == half), (slot >> 4) * 8 + (slot & 7), -1
        )
        owner_ref[:, 256 * half : 256 * half + 256] = ones_where(iota((1024, 256), 0) == place)
    column = jnp.transpose(jnp.broadcast_to(slot, (128, 256)).astype(F32))[:, 0:1].astype(I32)
    place = jnp.where(column >= 0, ((column & 15) >> 1) * 128 + (column >> 4), -1)
    rows_ref[...] = ones_where(iota((256, 1024), 1) == place)
    half_ref[...] = jnp.where((iota((256, 512), 1) >> 8) == (column & 1), 1.0, 0.0)

    lane = iota((1, 640), 1)
    plane = lane & 15
    group = jnp.where(plane >= 10, 1, 0)
    target = (
        ((lane >> 4) & 1) * 256
        + group * 128
        + (plane - 10 * group) * 12
        + 2 * (lane >> 7)
        + ((lane >> 5) & 3)
    )
    lanes_ref[...] = ones_where(iota((512, 640), 0) == target)

    row = iota((512, 1), 0)
    x = (row >> 5) & 3
    y = 2 * ((row >> 7) & 1) + ((row >> 4) & 1)
    z = 2 * (row >> 8) + (row & 1)
    channel = (row >> 1) & 7
    col = iota((512, 256), 1)
    for px in range(2):
        for py in range(2):
            parts = []
            for pz in range(2):
                i, j, k = x - px, y - py, z - pz
                good = (i >= 0) & (i < 3) & (j >= 0) & (j < 3) & (k >= 0) & (k < 3)
                tap = jnp.where(good, ((i * 3 + j) * 3 + k) * 8 + channel, -1)
                parts.append(ones_where(col == tap))
            block = dot_nn(jnp.concatenate(parts, axis=1), lift_ref[...])
            at = (px * 2 + py) * 128
            big_ref[:, at : at + 128] = (0.5 * block).astype(BF)

    eye = ones_where(iota((64, 64), 0) == iota((64, 64), 1))
    turned = dot_nt(eye, down_ref[...]).astype(BF)
    for a in range(2):
        for b in range(2):
            for d in range(2):
                for p in range(4):
                    at = ((2 * a + p // 2) * 4 + 2 * b + p % 2) * 256 + d * 128
                    taps_ref[2 * a + b, 64 * d : 64 * d + 64, 128 * p : 128 * p + 128] = turned[
                        :, at : at + 128
                    ]

    row, col = iota((256, 256), 0), iota((256, 256), 1)
    turn = ones_where(col == (row & 7) * 32 + (row >> 3))
    for g in range(8):
        part = dot_nn(turn, field_ref[8 * g : 8 * g + 8].reshape(256, 128))
        for uv in range(32):
            grad_ref[8 * g : 8 * g + 8, 128 * uv : 128 * uv + 128] = part[
                8 * uv : 8 * uv + 8
            ]


def lift_kernel(
    tile_ref,
    arrived_ref,
    weight_ref,
    bias_ref,
    cells_ref,
    rows_ref,
    half_ref,
    lanes_ref,
    big_ref,
    grad_ref,
    send_ref,
    pairs_ref,
    last_ref,
    sorted_ref,
    shallow_ref,
    deep_ref,
    end_ref,
    even_ref,
    odd_ref,
    cot_ref,
    sum_ref,
):
    a, b = tile_ref[0], tile_ref[1]

    row, col = iota((256, 256), 0), iota((256, 256), 1)
    turn = ones_where(col == (row & 31) * 8 + (row >> 5))
    for tile in range(5):
        for pair in range(2):
            block = jnp.concatenate(
                [
                    arrived_ref[32 * s : 32 * s + 32, 8 * tile : 8 * tile + 8].reshape(256, 128)
                    for s in (2 * pair, 2 * pair + 1)
                ],
                axis=1,
            )
            part = dot_nn(turn, block).astype(BF)
            for r in range(8):
                group, t = divmod(8 * tile + r, 20)
                lane = 128 * (2 * (t % 2) + group)
                for s in range(2):
                    at = 128 * (t // 2) + 32 * (2 * pair + s)
                    sorted_ref[at : at + 32, lane : lane + 128] = part[
                        32 * r : 32 * r + 32, 128 * s : 128 * s + 128
                    ]

    end_ref[...] = jnp.zeros((5, 16, 256), F32)
    first = iota((128, 640), 0) == 0
    for half in range(2):
        whole = dot_nn(sorted_ref[640 * half : 640 * half + 640, :], lanes_ref[...])
        for r in range(5):
            y2 = 5 * half + r
            part = whole[128 * r : 128 * r + 128]
            moved = jnp.where(first, 0.0, pltpu.roll(part, 1, 0)).astype(BF)
            now = part.astype(BF)
            for u in range(5):
                lane = 128 * u
                deep_ref[u, 128 * y2 : 128 * y2 + 128, :] = now[:, lane : lane + 128]
                shallow_ref[u, 128 * y2 : 128 * y2 + 128, :] = moved[:, lane : lane + 128]
                if y2 < 9:
                    end_ref[u, y2 : y2 + 1, 0:128] = part[127:128, lane : lane + 128]
                if y2 > 0:
                    end_ref[u, y2 - 1 : y2, 128:256] = part[127:128, lane : lane + 128]

    lane, channel = iota((64, 512), 1) & 255, iota((64, 512), 0)
    fold = ones_where(lane == jnp.where(channel < 56, channel + 200, channel + 64))
    pulled = (dot_nn(rows_ref[...], sorted_ref[0:1024, :]) * half_ref[...]).astype(BF)
    spread = dot_nt(fold, pulled) * weight_ref[...]
    added = dot_nt(jnp.concatenate(split(spread), axis=0), cells_ref[...])
    grown = (grad_ref[...] + added[0:64] + added[64:128]).astype(BF)
    cot_ref[0:64, :] = grown
    lane = iota((64, 128), 1)
    ends = jnp.zeros((64, 128), F32)
    for uv in range(32):
        piece = grown[:, 128 * uv : 128 * uv + 128].astype(F32)
        moved = pltpu.roll(piece, 1, 1)
        cot_ref[64:128, 128 * uv : 128 * uv + 128] = jnp.where(lane == 0, 0.0, moved).astype(BF)
        at = (uv // 8) * 16 + uv % 8
        ends = jnp.where(lane == at, pltpu.roll(piece, at + 1, 1), ends)

    bias = bias_ref[...]

    def active(h):
        h = h + bias
        return h + h * jnp.tanh(h * (2.0 * ROOT_2_PI + (8.0 * 0.044715 * ROOT_2_PI) * (h * h)))

    lane = iota((16, 512), 1)
    start = jnp.where((iota((16, 512), 0) == 0) & (((lane >> 6) & 1) == 0), 0.0, 1.0)

    def multiply(n, out_ref):
        u = n // 3
        v = 3 * (n - 3 * u)
        near = pl.ds(pl.multiple_of(128 * v, 128), 384)
        far = pl.ds(pl.multiple_of(128 * v + 128, 128), 384)
        both = jnp.concatenate(
            [shallow_ref[u, near], shallow_ref[u, far], deep_ref[u, near], deep_ref[u, far]], axis=1
        )
        out_ref[...] = dot_nn(both, big_ref[...])

    def activate(n, in_ref):
        u = n // 3
        v = 3 * (n - 3 * u)
        for t in range(3):
            value = active(in_ref[128 * t : 128 * t + 128, :])
            pairs_ref[u, v + t] = value.astype(BF)
            pairs_ref[u, v + t, 0:16, :] = (value[0:16] * start).astype(BF)

    multiply(0, even_ref)

    def strips(n, carry):
        multiply(2 * n + 1, odd_ref)
        activate(2 * n, even_ref)
        multiply(2 * n + 2, even_ref)
        activate(2 * n + 1, odd_ref)
        return carry

    lax.fori_loop(0, 7, strips, 0)
    activate(14, even_ref)

    def clear(where, u, v, low):
        @pl.when(where)
        def _():
            for lane in low:
                shape = (5 if u is None else 1, 9 if v is None else 1, 128, 128)
                pairs_ref[
                    slice(None) if u is None else slice(u, u + 1),
                    slice(None) if v is None else slice(v, v + 1),
                    :,
                    lane : lane + 128,
                ] = jnp.zeros(shape, BF)

    clear(a == 0, 0, None, (0, 128))
    clear(a == 15, 4, None, (256, 384))
    clear(b == 0, None, 0, (0, 256))
    clear(b == 7, None, 8, (128, 384))

    row, lane = iota((80, 512), 0), iota((80, 512), 1)
    px, py, pz = lane >> 8, (lane >> 7) & 1, (lane >> 6) & 1
    u, v = row >> 4, row & 15
    keep = (
        (pz == 0)
        & (v < 9)
        & ~((a == 0) & (u == 0) & (px == 0))
        & ~((a == 15) & (u == 4) & (px == 1))
        & ~((b == 0) & (v == 0) & (py == 0))
        & ~((b == 7) & (v == 8) & (py == 1))
    )
    ending = active(dot_nn(end_ref[...].reshape(80, 256).astype(BF), big_ref[0:256, :]))
    ending = jnp.where(keep, ending, 0.0)
    last = jnp.concatenate([ending, jnp.zeros((48, 512), F32)], axis=0).astype(BF)
    last_ref[...] = last

    none = jnp.zeros((128, 128), BF)
    edges = []
    for shift in (0, 1, 16, 17):
        edge = pltpu.roll(ends, shift, 1) if shift else ends
        edges += [none[0:64], edge.astype(BF)]
    sum_ref[...] = dot_nn(jnp.concatenate(edges, axis=0), last)
    for u in range(5):
        sides = [i for i in range(2) if 0 <= u - i < 4]
        rows = []
        for i in sides:
            cot = cot_ref[:, 1024 * (u - i) : 1024 * (u - i) + 1024]
            rows += [
                jnp.concatenate([cot, none], axis=1),
                jnp.concatenate([none, cot], axis=1),
            ]
        at = 256 * sides[0]
        sum_ref[at : at + 128 * len(rows), :] += dot_nn(
            jnp.concatenate(rows, axis=0), pairs_ref[u].reshape(1152, 512)
        )
    for r in range(32):
        for j in range(4):
            send_ref[4 * r + j] = sum_ref[16 * r : 16 * r + 16, 128 * j : 128 * j + 128].astype(BF)


def coarse_kernel(
    pairs_ref,
    last_ref,
    taps_ref,
    bias_ref,
    weight_ref,
    cells_ref,
    owner_ref,
    coarse_ref,
    feat_ref,
    wide_ref,
):
    lane = iota((64, 128), 1)
    edge = jnp.zeros((64, 128), F32)
    for i in range(2):
        for j in range(2):
            part = dot_nt(taps_ref[2 * i + j, 64:128, :], last_ref[...])
            shift = (128 - 16 * i - j) % 128
            edge = edge + (pltpu.roll(part, shift, 1) if shift else part)
    bias = bias_ref[...]

    def layer(u, carry):
        total = None
        for i in range(2):
            for j in range(2):
                group = pairs_ref[u + i, j : j + 8].reshape(1024, 512)
                part = dot_nt(taps_ref[2 * i + j], group)
                total = part if total is None else total + part
        for v in range(8):
            near = total[0:64, 128 * v : 128 * v + 128]
            deep = pltpu.roll(total[64:128, 128 * v : 128 * v + 128], 127, 1)
            end = pltpu.roll(edge, 127 - (16 * u + v), 1)
            value = near + jnp.where(lane == 127, end, deep) + bias
            at = pl.multiple_of(1024 * u + 128 * v, 128)
            wide_ref[:, pl.ds(at, 128)] = value
        return carry

    lax.fori_loop(0, 4, layer, 0)

    picked = dot_nn(wide_ref[...].astype(BF), cells_ref[...]) * weight_ref[...]
    feat = jnp.zeros((1024, 128), F32)
    none = jnp.zeros((64, 256), BF)
    for part in split(picked):
        twice = jnp.concatenate(
            [jnp.concatenate([part, none], axis=1), jnp.concatenate([none, part], axis=1)], axis=0
        )
        feat = feat + dot_nt(owner_ref[...], twice)
    feat_ref[...] = feat.astype(BF).reshape(128, 8, 128)

    row, col = iota((256, 256), 0), iota((256, 256), 1)
    turn = ones_where(col == (row & 31) * 8 + (row >> 5))
    for g in range(8):
        tall = jnp.concatenate(
            [wide_ref[8 * g : 8 * g + 8, 128 * uv : 128 * uv + 128] for uv in range(32)], axis=0
        )
        part = dot_nn(turn, tall.astype(BF)).astype(BF)
        coarse_ref[8 * g : 8 * g + 8] = part.reshape(8, 32, 128)


def sum_kernel(scale, parts_ref, feat_ref, out_ref):
    total = jnp.sum(parts_ref[...].astype(F32), axis=0) * scale
    out_ref[:, 0:16, :] = jnp.broadcast_to(total.astype(BF)[None], (128, 16, 128))
    out_ref[:, 16:24, :] = feat_ref[...]


def finish_kernel(arrived_ref, grad_ref, feat_ref):
    eye = ones_where(iota((128, 128), 0) == iota((128, 128), 1))
    for a in range(2):
        for b in range(2):
            for d in range(2):
                base = 4 * (4 * a + 2 * b + d)
                for p in range(4):
                    block = jnp.concatenate(
                        [arrived_ref[4 * (base + t) + p, 0:16, :] for t in range(4)], axis=0
                    )
                    tap = ((2 * a + p // 2) * 4 + 2 * b + p % 2) * 4 + 2 * d
                    grad_ref[64 * tap : 64 * tap + 128, :] = dot_nt(eye, block)
    feat = jnp.sum(arrived_ref[:, 16:24, :].astype(F32), axis=0)
    feat_ref[0:8, :] = feat[:, 0:64]
    feat_ref[8:16, :] = pltpu.roll(feat, 64, 1)[:, 0:64]


def call(kernel, outs, scratch=(), scalars=0, cost=0):
    extra = {}
    if scalars:
        extra["in_specs"] = [pl.BlockSpec(memory_space=pltpu.SMEM)] + [
            pl.BlockSpec(memory_space=pltpu.VMEM)
        ] * scalars
    return pl.pallas_call(
        kernel,
        out_shape=[jax.ShapeDtypeStruct(shape, dtype) for shape, dtype in outs],
        scratch_shapes=[pltpu.VMEM(shape, dtype) for shape, dtype in scratch],
        compiler_params=pltpu.CompilerParams(vmem_limit_bytes=56 << 20),
        cost_estimate=pl.CostEstimate(flops=cost, bytes_accessed=1 << 20, transcendentals=0),
        interpret=INTERPRET,
        **extra,
    )


def pack(fields, well_grad):
    return call(pack_kernel, [((16, 8, 40, 128), BF)], cost=1 << 31)(
        fields.reshape(16, 128, 128), well_grad
    )[0].reshape(128, 40, 128)


def prepare(perf_well, perf_cell, well_slot, w_lift, down_weight, field_grad):
    flat = jnp.pad(w_lift.reshape(216, 64), ((0, 40), (0, 0)))
    none = jnp.zeros_like(flat)
    lift = jnp.concatenate(
        [jnp.concatenate([flat, none], axis=1), jnp.concatenate([none, flat], axis=1)], axis=0
    )
    outs = [
        ((4096, 256), BF),
        ((256, 1024), BF),
        ((256, 512), F32),
        ((1024, 512), BF),
        ((512, 640), BF),
        ((512, 512), BF),
        ((4, 128, 512), BF),
        ((64, 4096), F32),
    ]
    return call(prep_kernel, outs, cost=1 << 32)(
        perf_well,
        perf_cell,
        well_slot.reshape(1, 2048),
        lift,
        down_weight.reshape(4096, 64),
        field_grad.reshape(64, 32, 128),
    )


def lift(tile, arrived, perf_weight, b_lift, cells, rows, half, lanes, big, grad):
    outs = [((128, 16, 128), BF), ((5, 9, 128, 512), BF), ((128, 512), BF)]
    scratch = [
        ((1280, 512), BF),
        ((5, 1280, 128), BF),
        ((5, 1280, 128), BF),
        ((5, 16, 256), F32),
        ((384, 512), F32),
        ((384, 512), F32),
        ((128, 4096), BF),
        ((512, 512), F32),
    ]
    return call(lift_kernel, outs, scratch, scalars=9, cost=1 << 33)(
        tile,
        arrived,
        perf_weight,
        jnp.tile(0.5 * b_lift, 8)[None, :],
        cells,
        rows,
        half,
        lanes,
        big,
        grad,
    )


def coarsen(pairs, last, taps, b_down, perf_weight, cells, owner):
    outs = [((64, 32, 128), BF), ((128, 8, 128), BF)]
    return call(coarse_kernel, outs, [((64, 4096), F32)], cost=1 << 33)(
        pairs, last, taps, b_down[:, None], perf_weight, cells, owner
    )


def exchange(blocks):
    return lax.all_to_all(blocks, AXES, split_axis=0, concat_axis=0, tiled=True)


def body(
    fields,
    w_lift,
    b_lift,
    down_weight,
    b_down,
    perf_well,
    perf_cell,
    perf_weight,
    well_slot,
    well_grad,
    field_grad,
):
    scale = 1.0 / math.sqrt(64 * 64 * 128)
    tile = jnp.stack([lax.axis_index("gx"), lax.axis_index("gy")]).astype(I32)
    arrived = exchange(pack(fields, well_grad))
    cells, rows, half, owner, lanes, big, taps, grad = prepare(
        perf_well, perf_cell, well_slot, w_lift, down_weight, field_grad
    )
    parts, pairs, last = lift(
        tile, arrived, perf_weight, b_lift, cells, rows, half, lanes, big, grad
    )
    parts = exchange(parts)
    coarse, feat = coarsen(pairs, last, taps, b_down, perf_weight, cells, owner)
    shared = call(
        lambda *refs: sum_kernel(scale, *refs), [((128, 24, 128), BF)], cost=1 << 20
    )(parts, feat)[0]
    shared = exchange(shared)
    down_grad, well_feat = call(
        finish_kernel, [((4096, 64), F32), ((16, 64), F32)], cost=1 << 28
    )(shared)
    return (
        coarse.reshape(64, 4, 8, 128),
        well_feat,
        down_grad.reshape(4, 4, 4, 64, 64),
    )


def solution(mesh):
    placed = (
        P(None, AXES, None, None),
        P(),
        P(),
        P(),
        P(),
        P(AXES, None),
        P(AXES, None),
        P(AXES, None),
        P(),
        P(AXES, None),
        P(None, "gx", "gy", None),
    )
    return jax.shard_map(
        body,
        mesh=mesh,
        in_specs=placed,
        out_specs=(P(None, "gx", "gy", None), P(AXES, None), P()),
        check_vma=False,
    )
```

```python
import math

import jax
import jax.numpy as jnp
from jax import lax
from jax.experimental import pallas as pl
from jax.experimental.pallas import tpu as pltpu
from jax.sharding import PartitionSpec as P

BF = jnp.bfloat16
F32 = jnp.float32
I32 = jnp.int32
AXES = ("gx", "gy")
INTERPRET = False
ROOM_LIFT = 58
ROOT_2_PI = math.sqrt(2.0 / math.pi)


def dot_nn(a, b):
    return lax.dot_general(a, b, (((1,), (0,)), ((), ())), preferred_element_type=F32)


def dot_nt(a, b):
    return lax.dot_general(a, b, (((1,), (1,)), ((), ())), preferred_element_type=F32)


def iota(shape, dim):
    return lax.broadcasted_iota(I32, shape, dim)


def ones_where(mask):
    return jnp.where(mask, 1.0, 0.0).astype(BF)


def split(x):
    high = x.astype(BF)
    return high, (x - high.astype(F32)).astype(BF)


def pack_kernel(fields_ref, wells_ref, out_ref):
    row = iota((320, 1), 0)
    b = (row * 205) >> 13
    rho = row - 40 * b
    group = jnp.where(rho >= 20, 1, 0)
    t = rho - 20 * group
    y = 16 * b - 2 + t
    target = jnp.where((y >= 0) & (y < 128), group * 128 + y, -1)
    windows = ones_where(iota((320, 256), 1) == target)
    empty = jnp.zeros((128, 128), BF)

    def plane(j):
        return jnp.concatenate([fields_ref[j], fields_ref[10 + j] if j < 6 else empty], axis=1)

    lined = jnp.concatenate(
        [
            dot_nt(windows, jnp.concatenate([plane(2 * j), plane(2 * j + 1)], axis=0)).astype(BF)
            for j in range(5)
        ],
        axis=1,
    )
    channel, lane = iota((64, 128), 0), iota((64, 128), 1)
    wells = wells_ref[...]
    placed = jnp.concatenate(
        [
            dot_nn(wells, ones_where((channel >= 56) & (lane == channel + 64))),
            dot_nn(wells, ones_where((channel < 56) & (lane == channel + 72))),
        ],
        axis=0,
    ).astype(BF)
    target = jnp.where(t < 16, 16 * group + t, -1)
    extra = dot_nn(ones_where(iota((320, 32), 1) == target), placed)
    extra = jnp.concatenate([extra] * 4, axis=1)
    for part in range(4):
        lane = iota((1, 512), 1)
        within = lane & 127
        which = (within * 171) >> 11
        x = (lane >> 7) * 8 + 32 * part - 2 + within - 12 * which
        target = jnp.where((which < 10) & (x >= 0) & (x < 128), which * 128 + x, -1)
        spread = ones_where(iota((1280, 512), 0) == target)
        blocks = (dot_nn(lined, spread) + extra).astype(BF)
        for a in range(4):
            out_ref[4 * part + a] = blocks[:, 128 * a : 128 * a + 128].reshape(8, 40, 128)


def prep_kernel(
    well_ref,
    cell_ref,
    table_ref,
    lift_ref,
    down_ref,
    field_ref,
    cells_ref,
    rows_ref,
    half_ref,
    owner_ref,
    lanes_ref,
    big_ref,
    taps_ref,
    grad_ref,
):
    well = well_ref[...]
    used = well >= 0
    cells_ref[...] = ones_where(iota((4096, 256), 0) == jnp.where(used, cell_ref[...], -1))
    matches = ones_where(iota((2048, 256), 0) == well)
    table = table_ref[...]
    row = iota((8, 2048), 0)
    digits = jnp.where(row == 0, table >> 4, jnp.where(row == 1, table & 15, 0))
    found = dot_nn(digits.astype(F32).astype(BF), matches)
    slot = jnp.where(used, (found[0:1] * 16.0 + found[1:2]).astype(I32), -1)
    for half in range(2):
        place = jnp.where(
            used & (((slot >> 3) & 1) == half), (slot >> 4) * 8 + (slot & 7), -1
        )
        owner_ref[:, 256 * half : 256 * half + 256] = ones_where(iota((1024, 256), 0) == place)
    column = jnp.transpose(jnp.broadcast_to(slot, (128, 256)).astype(F32))[:, 0:1].astype(I32)
    place = jnp.where(column >= 0, ((column & 15) >> 1) * 128 + (column >> 4), -1)
    rows_ref[...] = ones_where(iota((256, 1024), 1) == place)
    half_ref[...] = jnp.where((iota((256, 512), 1) >> 8) == (column & 1), 1.0, 0.0)

    lane = iota((1, 640), 1)
    plane = lane & 15
    group = jnp.where(plane >= 10, 1, 0)
    target = (
        ((lane >> 4) & 1) * 256
        + group * 128
        + (plane - 10 * group) * 12
        + 2 * (lane >> 7)
        + ((lane >> 5) & 3)
    )
    lanes_ref[...] = ones_where(iota((512, 640), 0) == target)

    row = iota((512, 1), 0)
    x = (row >> 5) & 3
    y = 2 * ((row >> 7) & 1) + ((row >> 4) & 1)
    z = 2 * (row >> 8) + (row & 1)
    channel = (row >> 1) & 7
    col = iota((512, 256), 1)
    for px in range(2):
        for py in range(2):
            parts = []
            for pz in range(2):
                i, j, k = x - px, y - py, z - pz
                good = (i >= 0) & (i < 3) & (j >= 0) & (j < 3) & (k >= 0) & (k < 3)
                tap = jnp.where(good, ((i * 3 + j) * 3 + k) * 8 + channel, -1)
                parts.append(ones_where(col == tap))
            block = dot_nn(jnp.concatenate(parts, axis=1), lift_ref[...])
            at = (px * 2 + py) * 128
            big_ref[:, at : at + 128] = (0.5 * block).astype(BF)

    for a in range(2):
        for b in range(2):
            for p in range(4):
                at = ((2 * a + p // 2) * 4 + 2 * b + p % 2) * 256
                taps_ref[
                    128 * p : 128 * p + 128, 128 * (2 * a + b) : 128 * (2 * a + b) + 128
                ] = jnp.concatenate(
                    [down_ref[at : at + 128, :], down_ref[at + 128 : at + 256, :]], axis=1
                )

    row, col = iota((256, 256), 0), iota((256, 256), 1)
    turn = ones_where(col == (row & 7) * 32 + (row >> 3))
    for g in range(8):
        part = dot_nn(turn, field_ref[8 * g : 8 * g + 8].reshape(256, 128))
        for uv in range(32):
            grad_ref[8 * g : 8 * g + 8, 128 * uv : 128 * uv + 128] = part[
                8 * uv : 8 * uv + 8
            ]


def lift_kernel(
    tile_ref,
    arrived_ref,
    weight_ref,
    bias_ref,
    lanes_ref,
    cells_far,
    rows_far,
    half_far,
    big_far,
    grad_far,
    send_ref,
    last_ref,
    pairs_far,
    sorted_ref,
    shallow_ref,
    deep_ref,
    end_ref,
    even_ref,
    odd_ref,
    cot_ref,
    sum_ref,
    pairs_ref,
    cells_ref,
    rows_ref,
    half_ref,
    big_ref,
    grad_ref,
    arrive,
    leave,
):
    a, b = tile_ref[0], tile_ref[1]
    fetch = [
        pltpu.make_async_copy(source, target, arrive.at[n])
        for n, (source, target) in enumerate(
            [
                (rows_far, rows_ref),
                (half_far, half_ref),
                (cells_far, cells_ref),
                (grad_far, grad_ref),
                (big_far, big_ref),
            ]
        )
    ]
    for copy in fetch:
        copy.start()

    row, col = iota((256, 256), 0), iota((256, 256), 1)
    turn = ones_where(col == (row & 31) * 8 + (row >> 5))
    for tile in range(5):
        for pair in range(2):
            block = jnp.concatenate(
                [
                    arrived_ref[32 * s : 32 * s + 32, 8 * tile : 8 * tile + 8].reshape(256, 128)
                    for s in (2 * pair, 2 * pair + 1)
                ],
                axis=1,
            )
            part = dot_nn(turn, block).astype(BF)
            for r in range(8):
                group, t = divmod(8 * tile + r, 20)
                lane = 128 * (2 * (t % 2) + group)
                for s in range(2):
                    at = 128 * (t // 2) + 32 * (2 * pair + s)
                    sorted_ref[at : at + 32, lane : lane + 128] = part[
                        32 * r : 32 * r + 32, 128 * s : 128 * s + 128
                    ]

    end_ref[...] = jnp.zeros((5, 16, 256), F32)
    first = iota((128, 640), 0) == 0
    for half in range(2):
        whole = dot_nn(sorted_ref[640 * half : 640 * half + 640, :], lanes_ref[...])
        for r in range(5):
            y2 = 5 * half + r
            part = whole[128 * r : 128 * r + 128]
            moved = jnp.where(first, 0.0, pltpu.roll(part, 1, 0)).astype(BF)
            now = part.astype(BF)
            for u in range(5):
                lane = 128 * u
                deep_ref[u, 128 * y2 : 128 * y2 + 128, :] = now[:, lane : lane + 128]
                shallow_ref[u, 128 * y2 : 128 * y2 + 128, :] = moved[:, lane : lane + 128]
                if y2 < 9:
                    end_ref[u, y2 : y2 + 1, 0:128] = part[127:128, lane : lane + 128]
                if y2 > 0:
                    end_ref[u, y2 - 1 : y2, 128:256] = part[127:128, lane : lane + 128]

    for copy in fetch:
        copy.wait()
    lane, channel = iota((64, 512), 1) & 255, iota((64, 512), 0)
    fold = ones_where(lane == jnp.where(channel < 56, channel + 200, channel + 64))
    pulled = (dot_nn(rows_ref[...], sorted_ref[0:1024, :]) * half_ref[...]).astype(BF)
    spread = dot_nt(fold, pulled) * weight_ref[...]
    added = dot_nt(jnp.concatenate(split(spread), axis=0), cells_ref[...])
    grown = (grad_ref[...] + added[0:64] + added[64:128]).astype(BF)
    cot_ref[0:64, :] = grown
    lane = iota((64, 128), 1)
    ends = jnp.zeros((64, 128), F32)
    for uv in range(32):
        piece = grown[:, 128 * uv : 128 * uv + 128].astype(F32)
        moved = pltpu.roll(piece, 1, 1)
        cot_ref[64:128, 128 * uv : 128 * uv + 128] = jnp.where(lane == 0, 0.0, moved).astype(BF)
        at = (uv // 8) * 16 + uv % 8
        ends = jnp.where(lane == at, pltpu.roll(piece, at + 1, 1), ends)

    bias = bias_ref[...]

    def active(h):
        h = h + bias
        return h + h * jnp.tanh(h * (2.0 * ROOT_2_PI + (8.0 * 0.044715 * ROOT_2_PI) * (h * h)))

    lane = iota((16, 512), 1)
    start = jnp.where((iota((16, 512), 0) == 0) & (((lane >> 6) & 1) == 0), 0.0, 1.0)

    def multiply(n, out_ref):
        u = n // 3
        v = 3 * (n - 3 * u)
        near = pl.ds(pl.multiple_of(128 * v, 128), 384)
        far = pl.ds(pl.multiple_of(128 * v + 128, 128), 384)
        both = jnp.concatenate(
            [shallow_ref[u, near], shallow_ref[u, far], deep_ref[u, near], deep_ref[u, far]], axis=1
        )
        out_ref[...] = dot_nn(both, big_ref[...])

    def activate(n, in_ref):
        u = n // 3
        v = 3 * (n - 3 * u)
        for t in range(3):
            value = active(in_ref[128 * t : 128 * t + 128, :])
            pairs_ref[u, v + t] = value.astype(BF)
            pairs_ref[u, v + t, 0:16, :] = (value[0:16] * start).astype(BF)

    multiply(0, even_ref)

    def strips(n, carry):
        multiply(2 * n + 1, odd_ref)
        activate(2 * n, even_ref)
        multiply(2 * n + 2, even_ref)
        activate(2 * n + 1, odd_ref)
        return carry

    lax.fori_loop(0, 7, strips, 0)
    activate(14, even_ref)

    def clear(where, u, v, low):
        @pl.when(where)
        def _():
            for lane in low:
                shape = (5 if u is None else 1, 9 if v is None else 1, 128, 128)
                pairs_ref[
                    slice(None) if u is None else slice(u, u + 1),
                    slice(None) if v is None else slice(v, v + 1),
                    :,
                    lane : lane + 128,
                ] = jnp.zeros(shape, BF)

    clear(a == 0, 0, None, (0, 128))
    clear(a == 15, 4, None, (256, 384))
    clear(b == 0, None, 0, (0, 256))
    clear(b == 7, None, 8, (128, 384))

    stores = [
        pltpu.make_async_copy(pairs_ref.at[u], pairs_far.at[u], leave.at[u]) for u in range(5)
    ]
    for copy in stores:
        copy.start()

    row, lane = iota((80, 512), 0), iota((80, 512), 1)
    px, py, pz = lane >> 8, (lane >> 7) & 1, (lane >> 6) & 1
    u, v = row >> 4, row & 15
    keep = (
        (pz == 0)
        & (v < 9)
        & ~((a == 0) & (u == 0) & (px == 0))
        & ~((a == 15) & (u == 4) & (px == 1))
        & ~((b == 0) & (v == 0) & (py == 0))
        & ~((b == 7) & (v == 8) & (py == 1))
    )
    ending = active(dot_nn(end_ref[...].reshape(80, 256).astype(BF), big_ref[0:256, :]))
    ending = jnp.where(keep, ending, 0.0)
    last = jnp.concatenate([ending, jnp.zeros((48, 512), F32)], axis=0).astype(BF)
    last_ref[...] = last

    none = jnp.zeros((128, 128), BF)
    edges = []
    for shift in (0, 1, 16, 17):
        edge = pltpu.roll(ends, shift, 1) if shift else ends
        edges += [none[0:64], edge.astype(BF)]
    sum_ref[...] = dot_nn(jnp.concatenate(edges, axis=0), last)
    for u in range(5):
        sides = [i for i in range(2) if 0 <= u - i < 4]
        rows = []
        for i in sides:
            cot = cot_ref[:, 1024 * (u - i) : 1024 * (u - i) + 1024]
            rows += [
                jnp.concatenate([cot, none], axis=1),
                jnp.concatenate([none, cot], axis=1),
            ]
        at = 256 * sides[0]
        sum_ref[at : at + 128 * len(rows), :] += dot_nn(
            jnp.concatenate(rows, axis=0), pairs_ref[u].reshape(1152, 512)
        )
    for r in range(32):
        for j in range(4):
            send_ref[4 * r + j] = sum_ref[16 * r : 16 * r + 16, 128 * j : 128 * j + 128].astype(BF)
    for copy in stores:
        copy.wait()


def coarse_kernel(
    taps_ref,
    last_ref,
    bias_ref,
    weight_ref,
    pairs_far,
    cells_far,
    owner_far,
    coarse_ref,
    feat_ref,
    wide_ref,
    tall_ref,
    first_ref,
    second_ref,
    third_ref,
    pairs_ref,
    cells_ref,
    owner_ref,
    arrive,
):
    fetch = [
        pltpu.make_async_copy(pairs_far.at[u], pairs_ref.at[u], arrive.at[u]) for u in range(5)
    ]
    fetch += [
        pltpu.make_async_copy(cells_far, cells_ref, arrive.at[5]),
        pltpu.make_async_copy(owner_far, owner_ref, arrive.at[6]),
    ]
    for copy in fetch:
        copy.start()

    edges = dot_nn(last_ref[...], taps_ref[...])
    edge = edges[:, 0:128]
    for n, shift in enumerate((127, 112, 111)):
        edge = edge + pltpu.roll(edges[:, 128 * n + 128 : 128 * n + 256], shift, 0)
    bias = bias_ref[...]
    bottom = iota((128, 128), 0) == 127
    slots = (first_ref, second_ref, third_ref)
    for u in range(5):
        fetch[u].wait()
        slots[u % 3][...] = dot_nn(pairs_ref[u].reshape(1152, 512), taps_ref[...])
        if u == 0:
            continue
        near, far = slots[(u - 1) % 3], slots[u % 3]
        for v in range(8):
            at = 128 * v
            total = (near[at : at + 128, 0:128] + near[at + 128 : at + 256, 128:256]) + (
                far[at : at + 128, 256:384] + far[at + 128 : at + 256, 384:512]
            )
            row = 16 * (u - 1) + v
            deep = jnp.where(bottom, edge[row : row + 1], pltpu.roll(total, 127, 0))
            value = total + pltpu.roll(deep, 64, 1) + bias
            at = 1024 * (u - 1) + 128 * v
            tall_ref[at : at + 128, :] = value.astype(BF)

    eye = ones_where(iota((64, 128), 0) == iota((64, 128), 1))
    wide_ref[...] = dot_nt(eye, tall_ref[...])
    fetch[5].wait()
    fetch[6].wait()
    picked = dot_nn(wide_ref[...].astype(BF), cells_ref[...]) * weight_ref[...]
    feat = jnp.zeros((1024, 128), F32)
    none = jnp.zeros((64, 256), BF)
    for part in split(picked):
        twice = jnp.concatenate(
            [jnp.concatenate([part, none], axis=1), jnp.concatenate([none, part], axis=1)], axis=0
        )
        feat = feat + dot_nt(owner_ref[...], twice)
    feat_ref[...] = feat.astype(BF).reshape(128, 8, 128)

    row, col = iota((256, 256), 0), iota((256, 256), 1)
    turn = ones_where(col == (row & 31) * 8 + (row >> 5))
    for g in range(8):
        tall = jnp.concatenate(
            [wide_ref[8 * g : 8 * g + 8, 128 * uv : 128 * uv + 128] for uv in range(32)], axis=0
        )
        part = dot_nn(turn, tall.astype(BF)).astype(BF)
        coarse_ref[8 * g : 8 * g + 8] = part.reshape(8, 32, 128)


def sum_kernel(scale, parts_ref, feat_ref, out_ref):
    total = jnp.sum(parts_ref[...].astype(F32), axis=0) * scale
    out_ref[:, 0:16, :] = jnp.broadcast_to(total.astype(BF)[None], (128, 16, 128))
    out_ref[:, 16:24, :] = feat_ref[...]


def finish_kernel(arrived_ref, grad_ref, feat_ref):
    eye = ones_where(iota((128, 128), 0) == iota((128, 128), 1))
    for a in range(2):
        for b in range(2):
            for d in range(2):
                base = 4 * (4 * a + 2 * b + d)
                for p in range(4):
                    block = jnp.concatenate(
                        [arrived_ref[4 * (base + t) + p, 0:16, :] for t in range(4)], axis=0
                    )
                    tap = ((2 * a + p // 2) * 4 + 2 * b + p % 2) * 4 + 2 * d
                    grad_ref[64 * tap : 64 * tap + 128, :] = dot_nt(eye, block)
    feat = jnp.sum(arrived_ref[:, 16:24, :].astype(F32), axis=0)
    feat_ref[0:8, :] = feat[:, 0:64]
    feat_ref[8:16, :] = pltpu.roll(feat, 64, 1)[:, 0:64]


VMEM, SMEM, HBM = pltpu.VMEM, pltpu.SMEM, pltpu.HBM


def call(kernel, outs, scratch=(), spaces=None, semaphores=(), cost=0, room=56):
    extra = {}
    if spaces is not None:
        places = [pl.BlockSpec(memory_space=space) for space in spaces]
        extra = {"in_specs": places[: -len(outs)], "out_specs": places[-len(outs) :]}
    return pl.pallas_call(
        kernel,
        out_shape=[jax.ShapeDtypeStruct(shape, dtype) for shape, dtype in outs],
        scratch_shapes=[pltpu.VMEM(shape, dtype) for shape, dtype in scratch]
        + [pltpu.SemaphoreType.DMA((count,)) for count in semaphores],
        compiler_params=pltpu.CompilerParams(vmem_limit_bytes=room << 20),
        cost_estimate=pl.CostEstimate(flops=cost, bytes_accessed=1 << 20, transcendentals=0),
        interpret=INTERPRET,
        **extra,
    )


def pack(fields, well_grad):
    return call(pack_kernel, [((16, 8, 40, 128), BF)], cost=1 << 31)(
        fields.reshape(16, 128, 128), well_grad
    )[0].reshape(128, 40, 128)


def prepare(perf_well, perf_cell, well_slot, w_lift, down_weight, field_grad):
    flat = jnp.pad(w_lift.reshape(216, 64), ((0, 40), (0, 0)))
    none = jnp.zeros_like(flat)
    lift = jnp.concatenate(
        [jnp.concatenate([flat, none], axis=1), jnp.concatenate([none, flat], axis=1)], axis=0
    )
    outs = [
        ((4096, 256), BF),
        ((256, 1024), BF),
        ((256, 512), F32),
        ((1024, 512), BF),
        ((512, 640), BF),
        ((512, 512), BF),
        ((512, 512), BF),
        ((64, 4096), F32),
    ]
    return call(prep_kernel, outs, cost=1 << 32)(
        perf_well,
        perf_cell,
        well_slot.reshape(1, 2048),
        lift,
        down_weight.reshape(4096, 64),
        field_grad.reshape(64, 32, 128),
    )


def lift(tile, arrived, perf_weight, b_lift, cells, rows, half, lanes, big, grad):
    outs = [((128, 16, 128), BF), ((128, 512), BF), ((5, 9, 128, 512), BF)]
    scratch = [
        ((1280, 512), BF),
        ((5, 1280, 128), BF),
        ((5, 1280, 128), BF),
        ((5, 16, 256), F32),
        ((384, 512), F32),
        ((384, 512), F32),
        ((128, 4096), BF),
        ((512, 512), F32),
        ((5, 9, 128, 512), BF),
        ((4096, 256), BF),
        ((256, 1024), BF),
        ((256, 512), F32),
        ((512, 512), BF),
        ((64, 4096), F32),
    ]
    spaces = [SMEM] + [VMEM] * 4 + [HBM] * 5 + [VMEM, VMEM, HBM]
    bias = jnp.tile(0.5 * b_lift, 8)[None, :]
    return call(lift_kernel, outs, scratch, spaces, (5, 5), cost=1 << 33, room=ROOM_LIFT)(
        tile, arrived, perf_weight, bias, lanes, cells, rows, half, big, grad
    )


def coarsen(pairs, last, taps, b_down, perf_weight, cells, owner):
    outs = [((64, 32, 128), BF), ((128, 8, 128), BF)]
    scratch = [
        ((64, 4096), F32),
        ((4096, 128), BF),
        ((1152, 512), F32),
        ((1152, 512), F32),
        ((1152, 512), F32),
        ((5, 9, 128, 512), BF),
        ((4096, 256), BF),
        ((1024, 512), BF),
    ]
    spaces = [VMEM] * 4 + [HBM] * 3 + [VMEM] * 2
    bias = jnp.tile(b_down, 2)[None, :]
    return call(coarse_kernel, outs, scratch, spaces, (7,), cost=1 << 33)(
        taps, last, bias, perf_weight, pairs, cells, owner
    )


def exchange(blocks):
    return lax.all_to_all(blocks, AXES, split_axis=0, concat_axis=0, tiled=True)


def body(
    fields,
    w_lift,
    b_lift,
    down_weight,
    b_down,
    perf_well,
    perf_cell,
    perf_weight,
    well_slot,
    well_grad,
    field_grad,
):
    scale = 1.0 / math.sqrt(64 * 64 * 128)
    tile = jnp.stack([lax.axis_index("gx"), lax.axis_index("gy")]).astype(I32)
    arrived = exchange(pack(fields, well_grad))
    cells, rows, half, owner, lanes, big, taps, grad = prepare(
        perf_well, perf_cell, well_slot, w_lift, down_weight, field_grad
    )
    parts, last, pairs = lift(
        tile, arrived, perf_weight, b_lift, cells, rows, half, lanes, big, grad
    )
    parts = exchange(parts)
    coarse, feat = coarsen(pairs, last, taps, b_down, perf_weight, cells, owner)
    shared = call(
        lambda *refs: sum_kernel(scale, *refs), [((128, 24, 128), BF)], cost=1 << 20, room=8
    )(parts, feat)[0]
    shared = exchange(shared)
    down_grad, well_feat = call(
        finish_kernel, [((4096, 64), F32), ((16, 64), F32)], cost=1 << 28, room=8
    )(shared)
    return (
        coarse.reshape(64, 4, 8, 128),
        well_feat,
        down_grad.reshape(4, 4, 4, 64, 64),
    )


def solution(mesh):
    placed = (
        P(None, AXES, None, None),
        P(),
        P(),
        P(),
        P(),
        P(AXES, None),
        P(AXES, None),
        P(AXES, None),
        P(),
        P(AXES, None),
        P(None, "gx", "gy", None),
    )
    return jax.shard_map(
        body,
        mesh=mesh,
        in_specs=placed,
        out_specs=(P(None, "gx", "gy", None), P(AXES, None), P()),
        check_vma=False,
    )
```

```python
import math

import jax
import jax.numpy as jnp
from jax import lax
from jax.experimental import pallas as pl
from jax.experimental.pallas import tpu as pltpu
from jax.sharding import PartitionSpec as P

BF = jnp.bfloat16
F32 = jnp.float32
I32 = jnp.int32
AXES = ("gx", "gy")
INTERPRET = False
ROOM_LIFT = 58
ROOT_2_PI = math.sqrt(2.0 / math.pi)


def dot_nn(a, b):
    return lax.dot_general(a, b, (((1,), (0,)), ((), ())), preferred_element_type=F32)


def dot_nt(a, b):
    return lax.dot_general(a, b, (((1,), (1,)), ((), ())), preferred_element_type=F32)


def iota(shape, dim):
    return lax.broadcasted_iota(I32, shape, dim)


def ones_where(mask):
    return jnp.where(mask, 1.0, 0.0).astype(BF)


def split(x):
    high = x.astype(BF)
    return high, (x - high.astype(F32)).astype(BF)


def pack_kernel(fields_ref, wells_ref, out_ref):
    row = iota((320, 1), 0)
    b = (row * 205) >> 13
    rho = row - 40 * b
    group = jnp.where(rho >= 20, 1, 0)
    t = rho - 20 * group
    y = 16 * b - 2 + t
    target = jnp.where((y >= 0) & (y < 128), group * 128 + y, -1)
    windows = ones_where(iota((320, 256), 1) == target)
    empty = jnp.zeros((64, 128), BF)

    def plane(j, x):
        return jnp.concatenate(
            [fields_ref[j, x : x + 64, :], fields_ref[10 + j, x : x + 64, :] if j < 6 else empty],
            axis=1,
        )

    channel, lane = iota((64, 128), 0), iota((64, 128), 1)
    wells = wells_ref[...]
    placed = jnp.concatenate(
        [
            dot_nn(wells, ones_where((channel >= 56) & (lane == channel + 64))),
            dot_nn(wells, ones_where((channel < 56) & (lane == channel + 72))),
        ],
        axis=0,
    ).astype(BF)
    target = jnp.where(t < 16, 16 * group + t, -1)
    extra = dot_nn(ones_where(iota((320, 32), 1) == target), placed)
    extra = jnp.concatenate([extra] * 4, axis=1)
    for part in range(4):
        origin = min(max(32 * part - 16, 0), 64)
        lined = jnp.concatenate(
            [
                dot_nt(
                    windows, jnp.concatenate([plane(4 * n + j, origin) for j in range(4)], axis=0)
                ).astype(BF)
                for n in range(2)
            ]
            + [
                dot_nt(
                    windows, jnp.concatenate([plane(8 + j, origin) for j in range(2)], axis=0)
                ).astype(BF)
            ],
            axis=1,
        )
        lane = iota((1, 512), 1)
        within = lane & 127
        which = (within * 171) >> 11
        x = (lane >> 7) * 8 + 32 * part - 2 + within - 12 * which
        target = jnp.where(
            (which < 10) & (x >= 0) & (x < 128), which * 64 + x - origin, -1
        )
        spread = ones_where(iota((640, 512), 0) == target)
        blocks = (dot_nn(lined, spread) + extra).astype(BF)
        for a in range(4):
            out_ref[4 * part + a] = blocks[:, 128 * a : 128 * a + 128].reshape(8, 40, 128)


def prep_kernel(
    well_ref,
    cell_ref,
    table_ref,
    lift_ref,
    down_ref,
    field_ref,
    cells_ref,
    rows_ref,
    half_ref,
    owner_ref,
    lanes_ref,
    big_ref,
    taps_ref,
    grad_ref,
):
    well = well_ref[...]
    used = well >= 0
    cells_ref[...] = ones_where(iota((4096, 256), 0) == jnp.where(used, cell_ref[...], -1))
    matches = ones_where(iota((2048, 256), 0) == well)
    table = table_ref[...]
    row = iota((8, 2048), 0)
    digits = jnp.where(row == 0, table >> 4, jnp.where(row == 1, table & 15, 0))
    found = dot_nn(digits.astype(F32).astype(BF), matches)
    slot = jnp.where(used, (found[0:1] * 16.0 + found[1:2]).astype(I32), -1)
    for half in range(2):
        place = jnp.where(
            used & (((slot >> 3) & 1) == half), (slot >> 4) * 8 + (slot & 7), -1
        )
        owner_ref[:, 256 * half : 256 * half + 256] = ones_where(iota((1024, 256), 0) == place)
    column = jnp.transpose(jnp.broadcast_to(slot, (128, 256)).astype(F32))[:, 0:1].astype(I32)
    place = jnp.where(column >= 0, ((column & 15) >> 1) * 128 + (column >> 4), -1)
    rows_ref[...] = ones_where(iota((256, 1024), 1) == place)
    half_ref[...] = jnp.where((iota((256, 512), 1) >> 8) == (column & 1), 1.0, 0.0)

    lane = iota((1, 640), 1)
    plane = lane & 15
    group = jnp.where(plane >= 10, 1, 0)
    target = (
        ((lane >> 4) & 1) * 256
        + group * 128
        + (plane - 10 * group) * 12
        + 2 * (lane >> 7)
        + ((lane >> 5) & 3)
    )
    lanes_ref[...] = ones_where(iota((512, 640), 0) == target)

    row = iota((512, 1), 0)
    x = (row >> 5) & 3
    y = 2 * ((row >> 7) & 1) + ((row >> 4) & 1)
    z = 2 * (row >> 8) + (row & 1)
    channel = (row >> 1) & 7
    col = iota((512, 256), 1)
    for px in range(2):
        for py in range(2):
            parts = []
            for pz in range(2):
                i, j, k = x - px, y - py, z - pz
                good = (i >= 0) & (i < 3) & (j >= 0) & (j < 3) & (k >= 0) & (k < 3)
                tap = jnp.where(good, ((i * 3 + j) * 3 + k) * 8 + channel, -1)
                parts.append(ones_where(col == tap))
            block = dot_nn(jnp.concatenate(parts, axis=1), lift_ref[...])
            at = (px * 2 + py) * 128
            big_ref[:, at : at + 128] = (0.5 * block).astype(BF)

    for a in range(2):
        for b in range(2):
            for p in range(4):
                at = ((2 * a + p // 2) * 4 + 2 * b + p % 2) * 256
                taps_ref[
                    128 * p : 128 * p + 128, 128 * (2 * a + b) : 128 * (2 * a + b) + 128
                ] = jnp.concatenate(
                    [down_ref[at : at + 128, :], down_ref[at + 128 : at + 256, :]], axis=1
                )

    row, col = iota((256, 256), 0), iota((256, 256), 1)
    turn = ones_where(col == (row & 7) * 32 + (row >> 3))
    for g in range(8):
        part = dot_nn(turn, field_ref[8 * g : 8 * g + 8].reshape(256, 128))
        for uv in range(32):
            grad_ref[8 * g : 8 * g + 8, 128 * uv : 128 * uv + 128] = part[
                8 * uv : 8 * uv + 8
            ]


def lift_kernel(
    tile_ref,
    arrived_ref,
    weight_ref,
    bias_ref,
    lanes_ref,
    cells_far,
    rows_far,
    half_far,
    big_far,
    grad_far,
    send_ref,
    last_ref,
    pairs_far,
    sorted_ref,
    shallow_ref,
    deep_ref,
    end_ref,
    even_ref,
    odd_ref,
    cot_ref,
    sum_ref,
    pairs_ref,
    cells_ref,
    rows_ref,
    half_ref,
    big_ref,
    grad_ref,
    arrive,
    leave,
):
    a, b = tile_ref[0], tile_ref[1]
    fetch = [
        pltpu.make_async_copy(source, target, arrive.at[n])
        for n, (source, target) in enumerate(
            [
                (rows_far, rows_ref),
                (half_far, half_ref),
                (cells_far, cells_ref),
                (grad_far, grad_ref),
                (big_far, big_ref),
            ]
        )
    ]
    for copy in fetch:
        copy.start()

    row, col = iota((256, 256), 0), iota((256, 256), 1)
    turn = ones_where(col == (row & 31) * 8 + (row >> 5))
    for tile in range(5):
        for pair in range(2):
            block = jnp.concatenate(
                [
                    arrived_ref[32 * s : 32 * s + 32, 8 * tile : 8 * tile + 8].reshape(256, 128)
                    for s in (2 * pair, 2 * pair + 1)
                ],
                axis=1,
            )
            part = dot_nn(turn, block).astype(BF)
            for r in range(8):
                group, t = divmod(8 * tile + r, 20)
                lane = 128 * (2 * (t % 2) + group)
                for s in range(2):
                    at = 128 * (t // 2) + 32 * (2 * pair + s)
                    sorted_ref[at : at + 32, lane : lane + 128] = part[
                        32 * r : 32 * r + 32, 128 * s : 128 * s + 128
                    ]

    end_ref[...] = jnp.zeros((5, 16, 256), F32)
    first = iota((128, 640), 0) == 0
    for half in range(2):
        whole = dot_nn(sorted_ref[640 * half : 640 * half + 640, :], lanes_ref[...])
        for r in range(5):
            y2 = 5 * half + r
            part = whole[128 * r : 128 * r + 128]
            moved = jnp.where(first, 0.0, pltpu.roll(part, 1, 0)).astype(BF)
            now = part.astype(BF)
            for u in range(5):
                lane = 128 * u
                deep_ref[u, 128 * y2 : 128 * y2 + 128, :] = now[:, lane : lane + 128]
                shallow_ref[u, 128 * y2 : 128 * y2 + 128, :] = moved[:, lane : lane + 128]
                if y2 < 9:
                    end_ref[u, y2 : y2 + 1, 0:128] = part[127:128, lane : lane + 128]
                if y2 > 0:
                    end_ref[u, y2 - 1 : y2, 128:256] = part[127:128, lane : lane + 128]

    for copy in fetch:
        copy.wait()
    lane, channel = iota((64, 512), 1) & 255, iota((64, 512), 0)
    fold = ones_where(lane == jnp.where(channel < 56, channel + 200, channel + 64))
    pulled = (dot_nn(rows_ref[...], sorted_ref[0:1024, :]) * half_ref[...]).astype(BF)
    spread = dot_nt(fold, pulled) * weight_ref[...]
    added = dot_nt(jnp.concatenate(split(spread), axis=0), cells_ref[...])
    grown = (grad_ref[...] + added[0:64] + added[64:128]).astype(BF)
    cot_ref[0:64, :] = grown
    lane = iota((64, 128), 1)
    ends = jnp.zeros((64, 128), F32)
    for uv in range(32):
        piece = grown[:, 128 * uv : 128 * uv + 128].astype(F32)
        moved = pltpu.roll(piece, 1, 1)
        cot_ref[64:128, 128 * uv : 128 * uv + 128] = jnp.where(lane == 0, 0.0, moved).astype(BF)
        at = (uv // 8) * 16 + uv % 8
        ends = jnp.where(lane == at, pltpu.roll(piece, at + 1, 1), ends)

    bias = bias_ref[...]

    def active(h):
        h = h + bias
        return h + h * jnp.tanh(h * (2.0 * ROOT_2_PI + (8.0 * 0.044715 * ROOT_2_PI) * (h * h)))

    lane = iota((16, 512), 1)
    start = jnp.where((iota((16, 512), 0) == 0) & (((lane >> 6) & 1) == 0), 0.0, 1.0)
    lane = iota((1, 512), 1)
    px, py = lane >> 8, (lane >> 7) & 1
    sides = {
        ("u", 0): jnp.where((a == 0) & (px == 0), 0.0, 1.0),
        ("u", 4): jnp.where((a == 15) & (px == 1), 0.0, 1.0),
        ("v", 0): jnp.where((b == 0) & (py == 0), 0.0, 1.0),
        ("v", 8): jnp.where((b == 7) & (py == 1), 0.0, 1.0),
    }

    def inside(value, u, v):
        for key in (("u", u), ("v", v)):
            if key in sides:
                value = value * sides[key]
        return value

    def multiply(u, t, out_ref):
        near, far = slice(384 * t, 384 * t + 384), slice(384 * t + 128, 384 * t + 512)
        both = jnp.concatenate(
            [shallow_ref[u, near], shallow_ref[u, far], deep_ref[u, near], deep_ref[u, far]], axis=1
        )
        out_ref[...] = dot_nn(both, big_ref[...])

    def activate(u, t, in_ref):
        for v in range(3 * t, 3 * t + 3):
            at = 128 * (v - 3 * t)
            value = inside(active(in_ref[at : at + 128, :]), u, v)
            pairs_ref[u, v, 0:16, :] = (value[0:16] * start).astype(BF)
            pairs_ref[u, v, 16:128, :] = value[16:128].astype(BF)

    row, lane = iota((80, 512), 0), iota((80, 512), 1)
    px, py, pz = lane >> 8, (lane >> 7) & 1, (lane >> 6) & 1
    u, v = row >> 4, row & 15
    keep = (
        (pz == 0)
        & (v < 9)
        & ~((a == 0) & (u == 0) & (px == 0))
        & ~((a == 15) & (u == 4) & (px == 1))
        & ~((b == 0) & (v == 0) & (py == 0))
        & ~((b == 7) & (v == 8) & (py == 1))
    )
    ending = active(dot_nn(end_ref[...].reshape(80, 256).astype(BF), big_ref[0:256, :]))
    ending = jnp.where(keep, ending, 0.0)
    last = jnp.concatenate([ending, jnp.zeros((48, 512), F32)], axis=0).astype(BF)
    last_ref[...] = last

    none = jnp.zeros((128, 128), BF)
    edges = []
    for shift in (0, 1, 16, 17):
        edge = pltpu.roll(ends, shift, 1) if shift else ends
        edges += [none[0:64], edge.astype(BF)]
    sum_ref[...] = dot_nn(jnp.concatenate(edges, axis=0), last)

    def gather(u):
        layers = [i for i in range(2) if 0 <= u - i < 4]
        rows = []
        for i in layers:
            cot = cot_ref[:, 1024 * (u - i) : 1024 * (u - i) + 1024]
            rows += [
                jnp.concatenate([cot, none], axis=1),
                jnp.concatenate([none, cot], axis=1),
            ]
        at = 256 * layers[0]
        sum_ref[at : at + 128 * len(rows), :] += dot_nn(
            jnp.concatenate(rows, axis=0), pairs_ref[u].reshape(1152, 512)
        )

    slots = (even_ref, odd_ref)
    stores = [
        pltpu.make_async_copy(pairs_ref.at[u], pairs_far.at[u], leave.at[u]) for u in range(5)
    ]
    for n in range(16):
        if n < 15:
            multiply(n // 3, n % 3, slots[n % 2])
        if n > 0:
            activate((n - 1) // 3, (n - 1) % 3, slots[(n - 1) % 2])
        if n > 3 and n % 3 == 1:
            gather(n // 3 - 1)
    for copy in stores:
        copy.start()
    gather(4)
    for r in range(32):
        for j in range(4):
            send_ref[4 * r + j] = sum_ref[16 * r : 16 * r + 16, 128 * j : 128 * j + 128].astype(BF)
    for copy in stores:
        copy.wait()


def coarse_kernel(
    taps_ref,
    last_ref,
    bias_ref,
    weight_ref,
    pairs_far,
    cells_far,
    owner_far,
    coarse_ref,
    feat_ref,
    wide_ref,
    tall_ref,
    first_ref,
    second_ref,
    third_ref,
    pairs_ref,
    cells_ref,
    owner_ref,
    arrive,
):
    fetch = [
        pltpu.make_async_copy(pairs_far.at[u], pairs_ref.at[u], arrive.at[u]) for u in range(5)
    ]
    fetch += [
        pltpu.make_async_copy(cells_far, cells_ref, arrive.at[5]),
        pltpu.make_async_copy(owner_far, owner_ref, arrive.at[6]),
    ]
    for copy in fetch:
        copy.start()

    edges = dot_nn(last_ref[...], taps_ref[...])
    edge = edges[:, 0:128]
    for n, shift in enumerate((127, 112, 111)):
        edge = edge + pltpu.roll(edges[:, 128 * n + 128 : 128 * n + 256], shift, 0)
    bias = bias_ref[...]
    bottom = iota((128, 128), 0) == 127
    slots = (first_ref, second_ref, third_ref)
    for u in range(5):
        fetch[u].wait()
        slots[u % 3][...] = dot_nn(pairs_ref[u].reshape(1152, 512), taps_ref[...])
        if u == 0:
            continue
        near, far = slots[(u - 1) % 3], slots[u % 3]
        for v in range(8):
            at = 128 * v
            total = (near[at : at + 128, 0:128] + near[at + 128 : at + 256, 128:256]) + (
                far[at : at + 128, 256:384] + far[at + 128 : at + 256, 384:512]
            )
            row = 16 * (u - 1) + v
            deep = jnp.where(bottom, edge[row : row + 1], pltpu.roll(total, 127, 0))
            value = total + pltpu.roll(deep, 64, 1) + bias
            at = 1024 * (u - 1) + 128 * v
            tall_ref[at : at + 128, :] = value.astype(BF)

    eye = ones_where(iota((64, 128), 0) == iota((64, 128), 1))
    wide_ref[...] = dot_nt(eye, tall_ref[...])
    fetch[5].wait()
    fetch[6].wait()
    picked = dot_nn(wide_ref[...].astype(BF), cells_ref[...]) * weight_ref[...]
    feat = jnp.zeros((1024, 128), F32)
    none = jnp.zeros((64, 256), BF)
    for part in split(picked):
        twice = jnp.concatenate(
            [jnp.concatenate([part, none], axis=1), jnp.concatenate([none, part], axis=1)], axis=0
        )
        feat = feat + dot_nt(owner_ref[...], twice)
    feat_ref[...] = feat.astype(BF).reshape(128, 8, 128)

    row, col = iota((256, 256), 0), iota((256, 256), 1)
    turn = ones_where(col == (row & 31) * 8 + (row >> 5))
    for g in range(8):
        tall = jnp.concatenate(
            [wide_ref[8 * g : 8 * g + 8, 128 * uv : 128 * uv + 128] for uv in range(32)], axis=0
        )
        part = dot_nn(turn, tall.astype(BF)).astype(BF)
        coarse_ref[8 * g : 8 * g + 8] = part.reshape(8, 32, 128)


def sum_kernel(scale, parts_ref, feat_ref, out_ref):
    total = jnp.sum(parts_ref[...].astype(F32), axis=0) * scale
    out_ref[:, 0:16, :] = jnp.broadcast_to(total.astype(BF)[None], (128, 16, 128))
    out_ref[:, 16:24, :] = feat_ref[...]


def finish_kernel(arrived_ref, grad_ref, feat_ref):
    eye = ones_where(iota((128, 128), 0) == iota((128, 128), 1))
    for a in range(2):
        for b in range(2):
            for d in range(2):
                base = 4 * (4 * a + 2 * b + d)
                for p in range(4):
                    block = jnp.concatenate(
                        [arrived_ref[4 * (base + t) + p, 0:16, :] for t in range(4)], axis=0
                    )
                    tap = ((2 * a + p // 2) * 4 + 2 * b + p % 2) * 4 + 2 * d
                    grad_ref[64 * tap : 64 * tap + 128, :] = dot_nt(eye, block)
    feat = jnp.sum(arrived_ref[:, 16:24, :].astype(F32), axis=0)
    feat_ref[0:8, :] = feat[:, 0:64]
    feat_ref[8:16, :] = pltpu.roll(feat, 64, 1)[:, 0:64]


VMEM, SMEM, HBM = pltpu.VMEM, pltpu.SMEM, pltpu.HBM


def call(kernel, outs, scratch=(), spaces=None, semaphores=(), cost=0, room=56):
    extra = {}
    if spaces is not None:
        places = [pl.BlockSpec(memory_space=space) for space in spaces]
        extra = {"in_specs": places[: -len(outs)], "out_specs": places[-len(outs) :]}
    return pl.pallas_call(
        kernel,
        out_shape=[jax.ShapeDtypeStruct(shape, dtype) for shape, dtype in outs],
        scratch_shapes=[pltpu.VMEM(shape, dtype) for shape, dtype in scratch]
        + [pltpu.SemaphoreType.DMA((count,)) for count in semaphores],
        compiler_params=pltpu.CompilerParams(vmem_limit_bytes=room << 20),
        cost_estimate=pl.CostEstimate(flops=cost, bytes_accessed=1 << 20, transcendentals=0),
        interpret=INTERPRET,
        **extra,
    )


def pack(fields, well_grad):
    return call(pack_kernel, [((16, 8, 40, 128), BF)], cost=1 << 31)(
        fields.reshape(16, 128, 128), well_grad
    )[0].reshape(128, 40, 128)


def prepare(perf_well, perf_cell, well_slot, w_lift, down_weight, field_grad):
    flat = jnp.pad(w_lift.reshape(216, 64), ((0, 40), (0, 0)))
    none = jnp.zeros_like(flat)
    lift = jnp.concatenate(
        [jnp.concatenate([flat, none], axis=1), jnp.concatenate([none, flat], axis=1)], axis=0
    )
    outs = [
        ((4096, 256), BF),
        ((256, 1024), BF),
        ((256, 512), F32),
        ((1024, 512), BF),
        ((512, 640), BF),
        ((512, 512), BF),
        ((512, 512), BF),
        ((64, 4096), F32),
    ]
    return call(prep_kernel, outs, cost=1 << 32)(
        perf_well,
        perf_cell,
        well_slot.reshape(1, 2048),
        lift,
        down_weight.reshape(4096, 64),
        field_grad.reshape(64, 32, 128),
    )


def lift(tile, arrived, perf_weight, b_lift, cells, rows, half, lanes, big, grad):
    outs = [((128, 16, 128), BF), ((128, 512), BF), ((5, 9, 128, 512), BF)]
    scratch = [
        ((1280, 512), BF),
        ((5, 1280, 128), BF),
        ((5, 1280, 128), BF),
        ((5, 16, 256), F32),
        ((384, 512), F32),
        ((384, 512), F32),
        ((128, 4096), BF),
        ((512, 512), F32),
        ((5, 9, 128, 512), BF),
        ((4096, 256), BF),
        ((256, 1024), BF),
        ((256, 512), F32),
        ((512, 512), BF),
        ((64, 4096), F32),
    ]
    spaces = [SMEM] + [VMEM] * 4 + [HBM] * 5 + [VMEM, VMEM, HBM]
    bias = jnp.tile(0.5 * b_lift, 8)[None, :]
    return call(lift_kernel, outs, scratch, spaces, (5, 5), cost=1 << 33, room=ROOM_LIFT)(
        tile, arrived, perf_weight, bias, lanes, cells, rows, half, big, grad
    )


def coarsen(pairs, last, taps, b_down, perf_weight, cells, owner):
    outs = [((64, 32, 128), BF), ((128, 8, 128), BF)]
    scratch = [
        ((64, 4096), F32),
        ((4096, 128), BF),
        ((1152, 512), F32),
        ((1152, 512), F32),
        ((1152, 512), F32),
        ((5, 9, 128, 512), BF),
        ((4096, 256), BF),
        ((1024, 512), BF),
    ]
    spaces = [VMEM] * 4 + [HBM] * 3 + [VMEM] * 2
    bias = jnp.tile(b_down, 2)[None, :]
    return call(coarse_kernel, outs, scratch, spaces, (7,), cost=1 << 33)(
        taps, last, bias, perf_weight, pairs, cells, owner
    )


def exchange(blocks):
    return lax.all_to_all(blocks, AXES, split_axis=0, concat_axis=0, tiled=True)


def body(
    fields,
    w_lift,
    b_lift,
    down_weight,
    b_down,
    perf_well,
    perf_cell,
    perf_weight,
    well_slot,
    well_grad,
    field_grad,
):
    scale = 1.0 / math.sqrt(64 * 64 * 128)
    tile = jnp.stack([lax.axis_index("gx"), lax.axis_index("gy")]).astype(I32)
    arrived = exchange(pack(fields, well_grad))
    cells, rows, half, owner, lanes, big, taps, grad = prepare(
        perf_well, perf_cell, well_slot, w_lift, down_weight, field_grad
    )
    parts, last, pairs = lift(
        tile, arrived, perf_weight, b_lift, cells, rows, half, lanes, big, grad
    )
    parts = exchange(parts)
    coarse, feat = coarsen(pairs, last, taps, b_down, perf_weight, cells, owner)
    shared = call(
        lambda *refs: sum_kernel(scale, *refs), [((128, 24, 128), BF)], cost=1 << 20, room=8
    )(parts, feat)[0]
    shared = exchange(shared)
    down_grad, well_feat = call(
        finish_kernel, [((4096, 64), F32), ((16, 64), F32)], cost=1 << 28, room=8
    )(shared)
    return (
        coarse.reshape(64, 4, 8, 128),
        well_feat,
        down_grad.reshape(4, 4, 4, 64, 64),
    )


def solution(mesh):
    placed = (
        P(None, AXES, None, None),
        P(),
        P(),
        P(),
        P(),
        P(AXES, None),
        P(AXES, None),
        P(AXES, None),
        P(),
        P(AXES, None),
        P(None, "gx", "gy", None),
    )
    return jax.shard_map(
        body,
        mesh=mesh,
        in_specs=placed,
        out_specs=(P(None, "gx", "gy", None), P(AXES, None), P()),
        check_vma=False,
    )
```

```python
import math

import jax
import jax.numpy as jnp
from jax import lax
from jax.experimental import pallas as pl
from jax.experimental.pallas import tpu as pltpu
from jax.sharding import PartitionSpec as P

BF = jnp.bfloat16
F32 = jnp.float32
I32 = jnp.int32
AXES = ("gx", "gy")
INTERPRET = False
ROOM_LIFT = 58
ROOT_2_PI = math.sqrt(2.0 / math.pi)


def dot_nn(a, b):
    return lax.dot_general(a, b, (((1,), (0,)), ((), ())), preferred_element_type=F32)


def dot_nt(a, b):
    return lax.dot_general(a, b, (((1,), (1,)), ((), ())), preferred_element_type=F32)


def iota(shape, dim):
    return lax.broadcasted_iota(I32, shape, dim)


def ones_where(mask):
    return jnp.where(mask, 1.0, 0.0).astype(BF)


def split(x):
    high = x.astype(BF)
    return high, (x - high.astype(F32)).astype(BF)


def pack_kernel(fields_ref, wells_ref, far_ref, out_ref, leave):
    row = iota((320, 1), 0)
    b = (row * 205) >> 13
    rho = row - 40 * b
    group = jnp.where(rho >= 20, 1, 0)
    t = rho - 20 * group
    y = 16 * b - 2 + t
    target = jnp.where((y >= 0) & (y < 128), group * 128 + y, -1)
    windows = ones_where(iota((320, 256), 1) == target)
    empty = jnp.zeros((64, 128), BF)

    def plane(j, x):
        return jnp.concatenate(
            [fields_ref[j, x : x + 64, :], fields_ref[10 + j, x : x + 64, :] if j < 6 else empty],
            axis=1,
        )

    channel, lane = iota((64, 128), 0), iota((64, 128), 1)
    wells = wells_ref[...]
    placed = jnp.concatenate(
        [
            dot_nn(wells, ones_where((channel >= 56) & (lane == channel + 64))),
            dot_nn(wells, ones_where((channel < 56) & (lane == channel + 72))),
        ],
        axis=0,
    ).astype(BF)
    target = jnp.where(t < 16, 16 * group + t, -1)
    extra = dot_nn(ones_where(iota((320, 32), 1) == target), placed)
    extra = jnp.concatenate([extra] * 4, axis=1)
    stores = [
        pltpu.make_async_copy(
            out_ref.at[4 * n : 4 * n + 4], far_ref.at[4 * n : 4 * n + 4], leave.at[n]
        )
        for n in range(4)
    ]
    for part in range(4):
        origin = min(max(32 * part - 16, 0), 64)
        lined = jnp.concatenate(
            [
                dot_nt(
                    windows, jnp.concatenate([plane(4 * n + j, origin) for j in range(4)], axis=0)
                ).astype(BF)
                for n in range(2)
            ]
            + [
                dot_nt(
                    windows, jnp.concatenate([plane(8 + j, origin) for j in range(2)], axis=0)
                ).astype(BF)
            ],
            axis=1,
        )
        lane = iota((1, 512), 1)
        within = lane & 127
        which = (within * 171) >> 11
        x = (lane >> 7) * 8 + 32 * part - 2 + within - 12 * which
        target = jnp.where(
            (which < 10) & (x >= 0) & (x < 128), which * 64 + x - origin, -1
        )
        spread = ones_where(iota((640, 512), 0) == target)
        blocks = (dot_nn(lined, spread) + extra).astype(BF)
        for a in range(4):
            out_ref[4 * part + a] = blocks[:, 128 * a : 128 * a + 128].reshape(8, 40, 128)
        stores[part].start()
    for copy in stores:
        copy.wait()


def prep_kernel(
    well_ref,
    cell_ref,
    table_ref,
    lift_ref,
    down_ref,
    field_ref,
    cells_ref,
    rows_ref,
    half_ref,
    owner_ref,
    lanes_ref,
    big_ref,
    taps_ref,
    grad_ref,
):
    well = well_ref[...]
    used = well >= 0
    cells_ref[...] = ones_where(iota((4096, 256), 0) == jnp.where(used, cell_ref[...], -1))
    matches = ones_where(iota((2048, 256), 0) == well)
    table = table_ref[...]
    row = iota((8, 2048), 0)
    digits = jnp.where(row == 0, table >> 4, jnp.where(row == 1, table & 15, 0))
    found = dot_nn(digits.astype(F32).astype(BF), matches)
    slot = jnp.where(used, (found[0:1] * 16.0 + found[1:2]).astype(I32), -1)
    for half in range(2):
        place = jnp.where(
            used & (((slot >> 3) & 1) == half), (slot >> 4) * 8 + (slot & 7), -1
        )
        owner_ref[:, 256 * half : 256 * half + 256] = ones_where(iota((1024, 256), 0) == place)
    column = jnp.transpose(jnp.broadcast_to(slot, (128, 256)).astype(F32))[:, 0:1].astype(I32)
    place = jnp.where(column >= 0, ((column & 15) >> 1) * 128 + (column >> 4), -1)
    rows_ref[...] = ones_where(iota((256, 1024), 1) == place)
    half_ref[...] = jnp.where((iota((256, 512), 1) >> 8) == (column & 1), 1.0, 0.0)

    lane = iota((1, 640), 1)
    plane = lane & 15
    group = jnp.where(plane >= 10, 1, 0)
    target = (
        ((lane >> 4) & 1) * 256
        + group * 128
        + (plane - 10 * group) * 12
        + 2 * (lane >> 7)
        + ((lane >> 5) & 3)
    )
    lanes_ref[...] = ones_where(iota((512, 640), 0) == target)

    row = iota((512, 1), 0)
    x = (row >> 5) & 3
    y = 2 * ((row >> 7) & 1) + ((row >> 4) & 1)
    z = 2 * (row >> 8) + (row & 1)
    channel = (row >> 1) & 7
    col = iota((512, 256), 1)
    for px in range(2):
        for py in range(2):
            parts = []
            for pz in range(2):
                i, j, k = x - px, y - py, z - pz
                good = (i >= 0) & (i < 3) & (j >= 0) & (j < 3) & (k >= 0) & (k < 3)
                tap = jnp.where(good, ((i * 3 + j) * 3 + k) * 8 + channel, -1)
                parts.append(ones_where(col == tap))
            block = dot_nn(jnp.concatenate(parts, axis=1), lift_ref[...])
            at = (px * 2 + py) * 128
            big_ref[:, at : at + 128] = (0.5 * block).astype(BF)

    for a in range(2):
        for b in range(2):
            for p in range(4):
                at = ((2 * a + p // 2) * 4 + 2 * b + p % 2) * 256
                taps_ref[
                    128 * p : 128 * p + 128, 128 * (2 * a + b) : 128 * (2 * a + b) + 128
                ] = jnp.concatenate(
                    [down_ref[at : at + 128, :], down_ref[at + 128 : at + 256, :]], axis=1
                )

    row, col = iota((256, 256), 0), iota((256, 256), 1)
    turn = ones_where(col == (row & 7) * 32 + (row >> 3))
    for g in range(8):
        part = dot_nn(turn, field_ref[8 * g : 8 * g + 8].reshape(256, 128))
        for uv in range(32):
            grad_ref[8 * g : 8 * g + 8, 128 * uv : 128 * uv + 128] = part[
                8 * uv : 8 * uv + 8
            ]


def lift_kernel(
    tile_ref,
    weight_ref,
    bias_ref,
    arrived_far,
    lanes_far,
    cells_far,
    rows_far,
    half_far,
    big_far,
    grad_far,
    send_ref,
    last_ref,
    pairs_far,
    sorted_ref,
    shallow_ref,
    deep_ref,
    end_ref,
    even_ref,
    odd_ref,
    cot_ref,
    sum_ref,
    pairs_ref,
    cells_ref,
    rows_ref,
    half_ref,
    big_ref,
    grad_ref,
    arrived_ref,
    lanes_ref,
    arrive,
    leave,
):
    a, b = tile_ref[0], tile_ref[1]
    fetch = [
        pltpu.make_async_copy(source, target, arrive.at[n])
        for n, (source, target) in enumerate(
            [
                (arrived_far.at[0:64], arrived_ref.at[0:64]),
                (arrived_far.at[64:128], arrived_ref.at[64:128]),
                (lanes_far, lanes_ref),
                (rows_far, rows_ref),
                (half_far, half_ref),
                (cells_far, cells_ref),
                (grad_far, grad_ref),
                (big_far, big_ref),
            ]
        )
    ]
    for copy in fetch:
        copy.start()

    row, col = iota((256, 256), 0), iota((256, 256), 1)
    turn = ones_where(col == (row & 31) * 8 + (row >> 5))
    for pair in range(2):
        fetch[pair].wait()
        for tile in range(5):
            block = jnp.concatenate(
                [
                    arrived_ref[32 * s : 32 * s + 32, 8 * tile : 8 * tile + 8].reshape(256, 128)
                    for s in (2 * pair, 2 * pair + 1)
                ],
                axis=1,
            )
            part = dot_nn(turn, block).astype(BF)
            for r in range(8):
                group, t = divmod(8 * tile + r, 20)
                lane = 128 * (2 * (t % 2) + group)
                for s in range(2):
                    at = 128 * (t // 2) + 32 * (2 * pair + s)
                    sorted_ref[at : at + 32, lane : lane + 128] = part[
                        32 * r : 32 * r + 32, 128 * s : 128 * s + 128
                    ]

    fetch[2].wait()
    end_ref[...] = jnp.zeros((5, 16, 256), F32)
    first = iota((128, 640), 0) == 0
    for half in range(2):
        whole = dot_nn(sorted_ref[640 * half : 640 * half + 640, :], lanes_ref[...])
        for r in range(5):
            y2 = 5 * half + r
            part = whole[128 * r : 128 * r + 128]
            moved = jnp.where(first, 0.0, pltpu.roll(part, 1, 0)).astype(BF)
            now = part.astype(BF)
            for u in range(5):
                lane = 128 * u
                deep_ref[u, 128 * y2 : 128 * y2 + 128, :] = now[:, lane : lane + 128]
                shallow_ref[u, 128 * y2 : 128 * y2 + 128, :] = moved[:, lane : lane + 128]
                if y2 < 9:
                    end_ref[u, y2 : y2 + 1, 0:128] = part[127:128, lane : lane + 128]
                if y2 > 0:
                    end_ref[u, y2 - 1 : y2, 128:256] = part[127:128, lane : lane + 128]

    for copy in fetch[3:]:
        copy.wait()
    lane, channel = iota((64, 512), 1) & 255, iota((64, 512), 0)
    fold = ones_where(lane == jnp.where(channel < 56, channel + 200, channel + 64))
    pulled = (dot_nn(rows_ref[...], sorted_ref[0:1024, :]) * half_ref[...]).astype(BF)
    spread = dot_nt(fold, pulled) * weight_ref[...]
    added = dot_nt(jnp.concatenate(split(spread), axis=0), cells_ref[...])
    grown = (grad_ref[...] + added[0:64] + added[64:128]).astype(BF)
    cot_ref[0:64, :] = grown
    lane = iota((64, 128), 1)
    ends = jnp.zeros((64, 128), F32)
    for uv in range(32):
        piece = grown[:, 128 * uv : 128 * uv + 128].astype(F32)
        moved = pltpu.roll(piece, 1, 1)
        cot_ref[64:128, 128 * uv : 128 * uv + 128] = jnp.where(lane == 0, 0.0, moved).astype(BF)
        at = (uv // 8) * 16 + uv % 8
        ends = jnp.where(lane == at, pltpu.roll(piece, at + 1, 1), ends)

    bias = bias_ref[...]

    def active(h):
        h = h + bias
        return h + h * jnp.tanh(h * (2.0 * ROOT_2_PI + (8.0 * 0.044715 * ROOT_2_PI) * (h * h)))

    lane = iota((16, 512), 1)
    start = jnp.where((iota((16, 512), 0) == 0) & (((lane >> 6) & 1) == 0), 0.0, 1.0)
    lane = iota((1, 512), 1)
    px, py = lane >> 8, (lane >> 7) & 1
    sides = {
        ("u", 0): jnp.where((a == 0) & (px == 0), 0.0, 1.0),
        ("u", 4): jnp.where((a == 15) & (px == 1), 0.0, 1.0),
        ("v", 0): jnp.where((b == 0) & (py == 0), 0.0, 1.0),
        ("v", 8): jnp.where((b == 7) & (py == 1), 0.0, 1.0),
    }

    def inside(value, u, v):
        for key in (("u", u), ("v", v)):
            if key in sides:
                value = value * sides[key]
        return value

    def multiply(u, t, out_ref):
        near, far = slice(384 * t, 384 * t + 384), slice(384 * t + 128, 384 * t + 512)
        both = jnp.concatenate(
            [shallow_ref[u, near], shallow_ref[u, far], deep_ref[u, near], deep_ref[u, far]], axis=1
        )
        out_ref[...] = dot_nn(both, big_ref[...])

    def activate(u, t, in_ref):
        for v in range(3 * t, 3 * t + 3):
            at = 128 * (v - 3 * t)
            value = inside(active(in_ref[at : at + 128, :]), u, v)
            pairs_ref[u, v, 0:16, :] = (value[0:16] * start).astype(BF)
            pairs_ref[u, v, 16:128, :] = value[16:128].astype(BF)

    row, lane = iota((80, 512), 0), iota((80, 512), 1)
    px, py, pz = lane >> 8, (lane >> 7) & 1, (lane >> 6) & 1
    u, v = row >> 4, row & 15
    keep = (
        (pz == 0)
        & (v < 9)
        & ~((a == 0) & (u == 0) & (px == 0))
        & ~((a == 15) & (u == 4) & (px == 1))
        & ~((b == 0) & (v == 0) & (py == 0))
        & ~((b == 7) & (v == 8) & (py == 1))
    )
    ending = active(dot_nn(end_ref[...].reshape(80, 256).astype(BF), big_ref[0:256, :]))
    ending = jnp.where(keep, ending, 0.0)
    last = jnp.concatenate([ending, jnp.zeros((48, 512), F32)], axis=0).astype(BF)
    last_ref[...] = last

    none = jnp.zeros((128, 128), BF)
    edges = []
    for shift in (0, 1, 16, 17):
        edge = pltpu.roll(ends, shift, 1) if shift else ends
        edges += [none[0:64], edge.astype(BF)]
    sum_ref[...] = dot_nn(jnp.concatenate(edges, axis=0), last)

    def gather(u):
        layers = [i for i in range(2) if 0 <= u - i < 4]
        rows = []
        for i in layers:
            cot = cot_ref[:, 1024 * (u - i) : 1024 * (u - i) + 1024]
            rows += [
                jnp.concatenate([cot, none], axis=1),
                jnp.concatenate([none, cot], axis=1),
            ]
        at = 256 * layers[0]
        sum_ref[at : at + 128 * len(rows), :] += dot_nn(
            jnp.concatenate(rows, axis=0), pairs_ref[u].reshape(1152, 512)
        )

    slots = (even_ref, odd_ref)
    stores = [
        pltpu.make_async_copy(pairs_ref.at[u], pairs_far.at[u], leave.at[u]) for u in range(5)
    ]
    for n in range(16):
        if n < 15:
            multiply(n // 3, n % 3, slots[n % 2])
        if n > 0:
            activate((n - 1) // 3, (n - 1) % 3, slots[(n - 1) % 2])
        if n > 0 and n % 3 == 0:
            stores[n // 3 - 1].start()
        if n > 3 and n % 3 == 1:
            gather(n // 3 - 1)
    gather(4)
    for r in range(32):
        for j in range(4):
            send_ref[4 * r + j] = sum_ref[16 * r : 16 * r + 16, 128 * j : 128 * j + 128].astype(BF)
    for copy in stores:
        copy.wait()


def coarse_kernel(
    taps_ref,
    last_ref,
    bias_ref,
    weight_ref,
    pairs_far,
    cells_far,
    owner_far,
    coarse_ref,
    feat_ref,
    wide_ref,
    tall_ref,
    first_ref,
    second_ref,
    third_ref,
    pairs_ref,
    cells_ref,
    owner_ref,
    arrive,
):
    fetch = [
        pltpu.make_async_copy(pairs_far.at[u], pairs_ref.at[u], arrive.at[u]) for u in range(5)
    ]
    fetch += [
        pltpu.make_async_copy(cells_far, cells_ref, arrive.at[5]),
        pltpu.make_async_copy(owner_far, owner_ref, arrive.at[6]),
    ]
    for copy in fetch:
        copy.start()

    edges = dot_nn(last_ref[...], taps_ref[...])
    edge = edges[:, 0:128]
    for n, shift in enumerate((127, 112, 111)):
        edge = edge + pltpu.roll(edges[:, 128 * n + 128 : 128 * n + 256], shift, 0)
    bias = bias_ref[...]
    bottom = iota((128, 128), 0) == 127
    slots = (first_ref, second_ref, third_ref)
    for u in range(5):
        fetch[u].wait()
        slots[u % 3][...] = dot_nn(pairs_ref[u].reshape(1152, 512), taps_ref[...])
        if u == 0:
            continue
        near, far = slots[(u - 1) % 3], slots[u % 3]
        for v in range(8):
            at = 128 * v
            total = (near[at : at + 128, 0:128] + near[at + 128 : at + 256, 128:256]) + (
                far[at : at + 128, 256:384] + far[at + 128 : at + 256, 384:512]
            )
            row = 16 * (u - 1) + v
            deep = jnp.where(bottom, edge[row : row + 1], pltpu.roll(total, 127, 0))
            value = total + pltpu.roll(deep, 64, 1) + bias
            at = 1024 * (u - 1) + 128 * v
            tall_ref[at : at + 128, :] = value.astype(BF)

    eye = ones_where(iota((64, 128), 0) == iota((64, 128), 1))
    wide_ref[...] = dot_nt(eye, tall_ref[...])
    fetch[5].wait()
    fetch[6].wait()
    picked = dot_nn(wide_ref[...].astype(BF), cells_ref[...]) * weight_ref[...]
    feat = jnp.zeros((1024, 128), F32)
    none = jnp.zeros((64, 256), BF)
    for part in split(picked):
        twice = jnp.concatenate(
            [jnp.concatenate([part, none], axis=1), jnp.concatenate([none, part], axis=1)], axis=0
        )
        feat = feat + dot_nt(owner_ref[...], twice)
    feat_ref[...] = feat.astype(BF).reshape(128, 8, 128)

    row, col = iota((256, 256), 0), iota((256, 256), 1)
    turn = ones_where(col == (row & 31) * 8 + (row >> 5))
    for g in range(8):
        tall = jnp.concatenate(
            [wide_ref[8 * g : 8 * g + 8, 128 * uv : 128 * uv + 128] for uv in range(32)], axis=0
        )
        part = dot_nn(turn, tall.astype(BF)).astype(BF)
        coarse_ref[8 * g : 8 * g + 8] = part.reshape(8, 32, 128)


def sum_kernel(scale, parts_ref, feat_ref, out_ref):
    total = jnp.sum(parts_ref[...].astype(F32), axis=0) * scale
    out_ref[:, 0:16, :] = jnp.broadcast_to(total.astype(BF)[None], (128, 16, 128))
    out_ref[:, 16:24, :] = feat_ref[...]


def finish_kernel(arrived_ref, grad_ref, feat_ref):
    tap = pl.program_id(0)
    a, px = tap // 2, tap % 2
    eye = ones_where(iota((128, 128), 0) == iota((128, 128), 1))
    for b in range(2):
        for py in range(2):
            for d in range(2):
                base = 16 * (4 * a + 2 * b + d) + 2 * px + py
                block = jnp.concatenate(
                    [arrived_ref[base + 4 * t, 0:16, :] for t in range(4)], axis=0
                )
                at = 256 * (2 * b + py) + 128 * d
                grad_ref[at : at + 128, :] = dot_nt(eye, block)

    @pl.when(tap == 0)
    def _():
        feat = jnp.sum(arrived_ref[:, 16:24, :].astype(F32), axis=0)
        feat_ref[0:8, :] = feat[:, 0:64]
        feat_ref[8:16, :] = pltpu.roll(feat, 64, 1)[:, 0:64]


VMEM, SMEM, HBM = pltpu.VMEM, pltpu.SMEM, pltpu.HBM


def call(kernel, outs, scratch=(), spaces=None, semaphores=(), cost=0, room=56):
    extra = {}
    if spaces is not None:
        places = [pl.BlockSpec(memory_space=space) for space in spaces]
        extra = {"in_specs": places[: -len(outs)], "out_specs": places[-len(outs) :]}
    return pl.pallas_call(
        kernel,
        out_shape=[jax.ShapeDtypeStruct(shape, dtype) for shape, dtype in outs],
        scratch_shapes=[pltpu.VMEM(shape, dtype) for shape, dtype in scratch]
        + [pltpu.SemaphoreType.DMA((count,)) for count in semaphores],
        compiler_params=pltpu.CompilerParams(vmem_limit_bytes=room << 20),
        cost_estimate=pl.CostEstimate(flops=cost, bytes_accessed=1 << 20, transcendentals=0),
        interpret=INTERPRET,
        **extra,
    )


def pack(fields, well_grad):
    outs = [((16, 8, 40, 128), BF)]
    return call(pack_kernel, outs, outs, [VMEM, VMEM, HBM], (4,), cost=1 << 31)(
        fields.reshape(16, 128, 128), well_grad
    )[0].reshape(128, 40, 128)


def prepare(perf_well, perf_cell, well_slot, w_lift, down_weight, field_grad):
    flat = jnp.pad(w_lift.reshape(216, 64), ((0, 40), (0, 0)))
    none = jnp.zeros_like(flat)
    lift = jnp.concatenate(
        [jnp.concatenate([flat, none], axis=1), jnp.concatenate([none, flat], axis=1)], axis=0
    )
    outs = [
        ((4096, 256), BF),
        ((256, 1024), BF),
        ((256, 512), F32),
        ((1024, 512), BF),
        ((512, 640), BF),
        ((512, 512), BF),
        ((512, 512), BF),
        ((64, 4096), F32),
    ]
    return call(prep_kernel, outs, cost=1 << 32)(
        perf_well,
        perf_cell,
        well_slot.reshape(1, 2048),
        lift,
        down_weight.reshape(4096, 64),
        field_grad.reshape(64, 32, 128),
    )


def lift(tile, arrived, perf_weight, b_lift, cells, rows, half, lanes, big, grad):
    outs = [((128, 16, 128), BF), ((128, 512), BF), ((5, 9, 128, 512), BF)]
    scratch = [
        ((1280, 512), BF),
        ((5, 1280, 128), BF),
        ((5, 1280, 128), BF),
        ((5, 16, 256), F32),
        ((384, 512), F32),
        ((384, 512), F32),
        ((128, 4096), BF),
        ((512, 512), F32),
        ((5, 9, 128, 512), BF),
        ((4096, 256), BF),
        ((256, 1024), BF),
        ((256, 512), F32),
        ((512, 512), BF),
        ((64, 4096), F32),
        ((128, 40, 128), BF),
        ((512, 640), BF),
    ]
    spaces = [SMEM] + [VMEM] * 2 + [HBM] * 7 + [VMEM, VMEM, HBM]
    bias = jnp.tile(0.5 * b_lift, 8)[None, :]
    return call(lift_kernel, outs, scratch, spaces, (8, 5), cost=1 << 33, room=ROOM_LIFT)(
        tile, perf_weight, bias, arrived, lanes, cells, rows, half, big, grad
    )


def coarsen(pairs, last, taps, b_down, perf_weight, cells, owner):
    outs = [((64, 32, 128), BF), ((128, 8, 128), BF)]
    scratch = [
        ((64, 4096), F32),
        ((4096, 128), BF),
        ((1152, 512), F32),
        ((1152, 512), F32),
        ((1152, 512), F32),
        ((5, 9, 128, 512), BF),
        ((4096, 256), BF),
        ((1024, 512), BF),
    ]
    spaces = [VMEM] * 4 + [HBM] * 3 + [VMEM] * 2
    bias = jnp.tile(b_down, 2)[None, :]
    return call(coarse_kernel, outs, scratch, spaces, (7,), cost=1 << 33)(
        taps, last, bias, perf_weight, pairs, cells, owner
    )


def finish(shared):
    return pl.pallas_call(
        finish_kernel,
        out_shape=[
            jax.ShapeDtypeStruct((4096, 64), F32),
            jax.ShapeDtypeStruct((16, 64), F32),
        ],
        grid=(4,),
        in_specs=[pl.BlockSpec((128, 24, 128), lambda i: (0, 0, 0))],
        out_specs=[
            pl.BlockSpec((1024, 64), lambda i: (i, 0)),
            pl.BlockSpec((16, 64), lambda i: (0, 0)),
        ],
        compiler_params=pltpu.CompilerParams(vmem_limit_bytes=8 << 20),
        interpret=INTERPRET,
    )(shared)


def exchange(blocks):
    return lax.all_to_all(blocks, AXES, split_axis=0, concat_axis=0, tiled=True)


def body(
    fields,
    w_lift,
    b_lift,
    down_weight,
    b_down,
    perf_well,
    perf_cell,
    perf_weight,
    well_slot,
    well_grad,
    field_grad,
):
    scale = 1.0 / math.sqrt(64 * 64 * 128)
    tile = jnp.stack([lax.axis_index("gx"), lax.axis_index("gy")]).astype(I32)
    arrived = exchange(pack(fields, well_grad))
    cells, rows, half, owner, lanes, big, taps, grad = prepare(
        perf_well, perf_cell, well_slot, w_lift, down_weight, field_grad
    )
    parts, last, pairs = lift(
        tile, arrived, perf_weight, b_lift, cells, rows, half, lanes, big, grad
    )
    parts = exchange(parts)
    coarse, feat = coarsen(pairs, last, taps, b_down, perf_weight, cells, owner)
    shared = call(
        lambda *refs: sum_kernel(scale, *refs), [((128, 24, 128), BF)], cost=1 << 20, room=8
    )(parts, feat)[0]
    shared = exchange(shared)
    down_grad, well_feat = finish(shared)
    return (
        coarse.reshape(64, 4, 8, 128),
        well_feat,
        down_grad.reshape(4, 4, 4, 64, 64),
    )


def solution(mesh):
    placed = (
        P(None, AXES, None, None),
        P(),
        P(),
        P(),
        P(),
        P(AXES, None),
        P(AXES, None),
        P(AXES, None),
        P(),
        P(AXES, None),
        P(None, "gx", "gy", None),
    )
    return jax.shard_map(
        body,
        mesh=mesh,
        in_specs=placed,
        out_specs=(P(None, "gx", "gy", None), P(AXES, None), P()),
        check_vma=False,
    )
```

```python
import math

import jax
import jax.numpy as jnp
from jax import lax
from jax.experimental import pallas as pl
from jax.experimental.pallas import tpu as pltpu
from jax.sharding import PartitionSpec as P

BF = jnp.bfloat16
F32 = jnp.float32
I32 = jnp.int32
AXES = ("gx", "gy")
INTERPRET = False
ROOM_LIFT = 58
ROOT_2_PI = math.sqrt(2.0 / math.pi)


def dot_nn(a, b):
    return lax.dot_general(a, b, (((1,), (0,)), ((), ())), preferred_element_type=F32)


def dot_nt(a, b):
    return lax.dot_general(a, b, (((1,), (1,)), ((), ())), preferred_element_type=F32)


def iota(shape, dim):
    return lax.broadcasted_iota(I32, shape, dim)


def ones_where(mask):
    return jnp.where(mask, 1.0, 0.0).astype(BF)


def split(x):
    high = x.astype(BF)
    return high, (x - high.astype(F32)).astype(BF)


def pack_kernel(fields_ref, wells_ref, far_ref, out_ref, leave):
    row = iota((320, 1), 0)
    b = (row * 205) >> 13
    rho = row - 40 * b
    group = jnp.where(rho >= 20, 1, 0)
    t = rho - 20 * group
    y = 16 * b - 2 + t
    target = jnp.where((y >= 0) & (y < 128), group * 128 + y, -1)
    windows = ones_where(iota((320, 256), 1) == target)
    empty = jnp.zeros((64, 128), BF)

    def plane(j, x):
        return jnp.concatenate(
            [fields_ref[j, x : x + 64, :], fields_ref[10 + j, x : x + 64, :] if j < 6 else empty],
            axis=1,
        )

    channel, lane = iota((64, 128), 0), iota((64, 128), 1)
    wells = wells_ref[...]
    placed = jnp.concatenate(
        [
            dot_nn(wells, ones_where((channel >= 56) & (lane == channel + 64))),
            dot_nn(wells, ones_where((channel < 56) & (lane == channel + 72))),
        ],
        axis=0,
    ).astype(BF)
    target = jnp.where(t < 16, 16 * group + t, -1)
    extra = dot_nn(ones_where(iota((320, 32), 1) == target), placed)
    extra = jnp.concatenate([extra] * 4, axis=1)
    stores = [
        pltpu.make_async_copy(
            out_ref.at[4 * n : 4 * n + 4], far_ref.at[4 * n : 4 * n + 4], leave.at[n]
        )
        for n in range(4)
    ]
    for part in range(4):
        origin = min(max(32 * part - 16, 0), 64)
        lined = jnp.concatenate(
            [
                dot_nt(
                    windows, jnp.concatenate([plane(4 * n + j, origin) for j in range(4)], axis=0)
                ).astype(BF)
                for n in range(2)
            ]
            + [
                dot_nt(
                    windows, jnp.concatenate([plane(8 + j, origin) for j in range(2)], axis=0)
                ).astype(BF)
            ],
            axis=1,
        )
        lane = iota((1, 512), 1)
        within = lane & 127
        which = (within * 171) >> 11
        x = (lane >> 7) * 8 + 32 * part - 2 + within - 12 * which
        target = jnp.where(
            (which < 10) & (x >= 0) & (x < 128), which * 64 + x - origin, -1
        )
        spread = ones_where(iota((640, 512), 0) == target)
        blocks = (dot_nn(lined, spread) + extra).astype(BF)
        for a in range(4):
            out_ref[4 * part + a] = blocks[:, 128 * a : 128 * a + 128].reshape(8, 40, 128)
        stores[part].start()
    for copy in stores:
        copy.wait()


def prep_kernel(
    well_ref,
    cell_ref,
    table_ref,
    lift_ref,
    down_ref,
    field_ref,
    cells_ref,
    rows_ref,
    half_ref,
    owner_ref,
    lanes_ref,
    big_ref,
    taps_ref,
    grad_ref,
):
    well = well_ref[...]
    used = well >= 0
    cells_ref[...] = ones_where(iota((4096, 256), 0) == jnp.where(used, cell_ref[...], -1))
    matches = ones_where(iota((2048, 256), 0) == well)
    table = table_ref[...]
    row = iota((8, 2048), 0)
    digits = jnp.where(row == 0, table >> 4, jnp.where(row == 1, table & 15, 0))
    found = dot_nn(digits.astype(F32).astype(BF), matches)
    slot = jnp.where(used, (found[0:1] * 16.0 + found[1:2]).astype(I32), -1)
    for half in range(2):
        place = jnp.where(
            used & (((slot >> 3) & 1) == half), (slot >> 4) * 8 + (slot & 7), -1
        )
        owner_ref[:, 256 * half : 256 * half + 256] = ones_where(iota((1024, 256), 0) == place)
    column = jnp.transpose(jnp.broadcast_to(slot, (128, 256)).astype(F32))[:, 0:1].astype(I32)
    place = jnp.where(column >= 0, ((column & 15) >> 1) * 128 + (column >> 4), -1)
    rows_ref[...] = ones_where(iota((256, 1024), 1) == place)
    half_ref[...] = ones_where((iota((256, 512), 1) >> 8) == (column & 1))

    lane = iota((1, 640), 1)
    plane = lane & 15
    group = jnp.where(plane >= 10, 1, 0)
    target = (
        ((lane >> 4) & 1) * 256
        + group * 128
        + (plane - 10 * group) * 12
        + 2 * (lane >> 7)
        + ((lane >> 5) & 3)
    )
    lanes_ref[...] = ones_where(iota((512, 640), 0) == target)

    row = iota((512, 1), 0)
    x = (row >> 5) & 3
    y = 2 * ((row >> 7) & 1) + ((row >> 4) & 1)
    z = 2 * (row >> 8) + (row & 1)
    channel = (row >> 1) & 7
    col = iota((512, 256), 1)
    for px in range(2):
        for py in range(2):
            parts = []
            for pz in range(2):
                i, j, k = x - px, y - py, z - pz
                good = (i >= 0) & (i < 3) & (j >= 0) & (j < 3) & (k >= 0) & (k < 3)
                tap = jnp.where(good, ((i * 3 + j) * 3 + k) * 8 + channel, -1)
                parts.append(ones_where(col == tap))
            block = dot_nn(jnp.concatenate(parts, axis=1), lift_ref[...])
            at = (px * 2 + py) * 128
            big_ref[:, at : at + 128] = (0.5 * block).astype(BF)

    for a in range(2):
        for b in range(2):
            for p in range(4):
                at = ((2 * a + p // 2) * 4 + 2 * b + p % 2) * 256
                taps_ref[
                    128 * p : 128 * p + 128, 128 * (2 * a + b) : 128 * (2 * a + b) + 128
                ] = jnp.concatenate(
                    [down_ref[at : at + 128, :], down_ref[at + 128 : at + 256, :]], axis=1
                )

    row, col = iota((256, 256), 0), iota((256, 256), 1)
    turn = ones_where(col == (row & 7) * 32 + (row >> 3))
    for g in range(8):
        part = dot_nn(turn, field_ref[8 * g : 8 * g + 8].reshape(256, 128))
        for uv in range(32):
            grad_ref[8 * g : 8 * g + 8, 128 * uv : 128 * uv + 128] = part[
                8 * uv : 8 * uv + 8
            ].astype(BF)


def lift_kernel(
    tile_ref,
    weight_ref,
    bias_ref,
    arrived_far,
    lanes_far,
    cells_far,
    rows_far,
    half_far,
    big_far,
    grad_far,
    send_ref,
    last_ref,
    pairs_far,
    sorted_ref,
    shallow_ref,
    deep_ref,
    end_ref,
    even_ref,
    odd_ref,
    cot_ref,
    sum_ref,
    pairs_ref,
    cells_ref,
    rows_ref,
    half_ref,
    big_ref,
    grad_ref,
    arrived_ref,
    lanes_ref,
    arrive,
    leave,
):
    a, b = tile_ref[0], tile_ref[1]
    fetch = [
        pltpu.make_async_copy(source, target, arrive.at[n])
        for n, (source, target) in enumerate(
            [
                (arrived_far.at[0:64], arrived_ref.at[0:64]),
                (arrived_far.at[64:128], arrived_ref.at[64:128]),
                (lanes_far, lanes_ref),
                (rows_far, rows_ref),
                (half_far, half_ref),
                (cells_far, cells_ref),
                (grad_far, grad_ref),
                (big_far, big_ref),
            ]
        )
    ]
    for copy in fetch:
        copy.start()

    row, col = iota((256, 256), 0), iota((256, 256), 1)
    turn = ones_where(col == (row & 31) * 8 + (row >> 5))
    for pair in range(2):
        fetch[pair].wait()
        for tile in range(5):
            block = jnp.concatenate(
                [
                    arrived_ref[32 * s : 32 * s + 32, 8 * tile : 8 * tile + 8].reshape(256, 128)
                    for s in (2 * pair, 2 * pair + 1)
                ],
                axis=1,
            )
            part = dot_nn(turn, block).astype(BF)
            for r in range(8):
                group, t = divmod(8 * tile + r, 20)
                lane = 128 * (2 * (t % 2) + group)
                for s in range(2):
                    at = 128 * (t // 2) + 32 * (2 * pair + s)
                    sorted_ref[at : at + 32, lane : lane + 128] = part[
                        32 * r : 32 * r + 32, 128 * s : 128 * s + 128
                    ]

    fetch[2].wait()
    end_ref[...] = jnp.zeros((5, 16, 256), F32)
    first = iota((128, 640), 0) == 0
    for half in range(2):
        whole = dot_nn(sorted_ref[640 * half : 640 * half + 640, :], lanes_ref[...])
        for r in range(5):
            y2 = 5 * half + r
            part = whole[128 * r : 128 * r + 128]
            moved = jnp.where(first, 0.0, pltpu.roll(part, 1, 0)).astype(BF)
            now = part.astype(BF)
            for u in range(5):
                lane = 128 * u
                deep_ref[u, 128 * y2 : 128 * y2 + 128, :] = now[:, lane : lane + 128]
                shallow_ref[u, 128 * y2 : 128 * y2 + 128, :] = moved[:, lane : lane + 128]
                if y2 < 9:
                    end_ref[u, y2 : y2 + 1, 0:128] = part[127:128, lane : lane + 128]
                if y2 > 0:
                    end_ref[u, y2 - 1 : y2, 128:256] = part[127:128, lane : lane + 128]

    for copy in fetch[3:]:
        copy.wait()
    lane, channel = iota((64, 512), 1) & 255, iota((64, 512), 0)
    fold = ones_where(lane == jnp.where(channel < 56, channel + 200, channel + 64))
    pulled = (dot_nn(rows_ref[...], sorted_ref[0:1024, :]) * half_ref[...].astype(F32)).astype(BF)
    spread = dot_nt(fold, pulled) * weight_ref[...]
    added = dot_nt(jnp.concatenate(split(spread), axis=0), cells_ref[...])
    grown = (grad_ref[...].astype(F32) + added[0:64] + added[64:128]).astype(BF)
    cot_ref[0:64, :] = grown
    lane = iota((64, 128), 1)
    ends = jnp.zeros((64, 128), F32)
    for uv in range(32):
        piece = grown[:, 128 * uv : 128 * uv + 128].astype(F32)
        moved = pltpu.roll(piece, 1, 1)
        cot_ref[64:128, 128 * uv : 128 * uv + 128] = jnp.where(lane == 0, 0.0, moved).astype(BF)
        at = (uv // 8) * 16 + uv % 8
        ends = jnp.where(lane == at, pltpu.roll(piece, at + 1, 1), ends)

    bias = bias_ref[...]

    def active(h):
        h = h + bias
        return h + h * jnp.tanh(h * (2.0 * ROOT_2_PI + (8.0 * 0.044715 * ROOT_2_PI) * (h * h)))

    lane = iota((16, 512), 1)
    start = jnp.where((iota((16, 512), 0) == 0) & (((lane >> 6) & 1) == 0), 0.0, 1.0)
    lane = iota((1, 512), 1)
    px, py = lane >> 8, (lane >> 7) & 1
    sides = {
        ("u", 0): jnp.where((a == 0) & (px == 0), 0.0, 1.0),
        ("u", 4): jnp.where((a == 15) & (px == 1), 0.0, 1.0),
        ("v", 0): jnp.where((b == 0) & (py == 0), 0.0, 1.0),
        ("v", 8): jnp.where((b == 7) & (py == 1), 0.0, 1.0),
    }

    def inside(value, u, v):
        for key in (("u", u), ("v", v)):
            if key in sides:
                value = value * sides[key]
        return value

    def multiply(u, t, out_ref):
        near, far = slice(384 * t, 384 * t + 384), slice(384 * t + 128, 384 * t + 512)
        both = jnp.concatenate(
            [shallow_ref[u, near], shallow_ref[u, far], deep_ref[u, near], deep_ref[u, far]], axis=1
        )
        out_ref[...] = dot_nn(both, big_ref[...])

    def activate(u, t, in_ref):
        for v in range(3 * t, 3 * t + 3):
            at = 128 * (v - 3 * t)
            value = inside(active(in_ref[at : at + 128, :]), u, v)
            pairs_ref[u, v, 0:16, :] = (value[0:16] * start).astype(BF)
            pairs_ref[u, v, 16:128, :] = value[16:128].astype(BF)

    row, lane = iota((80, 512), 0), iota((80, 512), 1)
    px, py, pz = lane >> 8, (lane >> 7) & 1, (lane >> 6) & 1
    u, v = row >> 4, row & 15
    keep = (
        (pz == 0)
        & (v < 9)
        & ~((a == 0) & (u == 0) & (px == 0))
        & ~((a == 15) & (u == 4) & (px == 1))
        & ~((b == 0) & (v == 0) & (py == 0))
        & ~((b == 7) & (v == 8) & (py == 1))
    )
    ending = active(dot_nn(end_ref[...].reshape(80, 256).astype(BF), big_ref[0:256, :]))
    ending = jnp.where(keep, ending, 0.0)
    last = jnp.concatenate([ending, jnp.zeros((48, 512), F32)], axis=0).astype(BF)
    last_ref[...] = last

    none = jnp.zeros((128, 128), BF)
    edges = []
    for shift in (0, 1, 16, 17):
        edge = pltpu.roll(ends, shift, 1) if shift else ends
        edges += [none[0:64], edge.astype(BF)]
    sum_ref[...] = dot_nn(jnp.concatenate(edges, axis=0), last)

    def gather(u):
        layers = [i for i in range(2) if 0 <= u - i < 4]
        rows = []
        for i in layers:
            cot = cot_ref[:, 1024 * (u - i) : 1024 * (u - i) + 1024]
            rows += [
                jnp.concatenate([cot, none], axis=1),
                jnp.concatenate([none, cot], axis=1),
            ]
        at = 256 * layers[0]
        sum_ref[at : at + 128 * len(rows), :] += dot_nn(
            jnp.concatenate(rows, axis=0), pairs_ref[u].reshape(1152, 512)
        )

    slots = (even_ref, odd_ref)
    stores = [
        pltpu.make_async_copy(pairs_ref.at[u], pairs_far.at[u], leave.at[u]) for u in range(5)
    ]
    for n in range(16):
        if n < 15:
            multiply(n // 3, n % 3, slots[n % 2])
        if n > 0:
            activate((n - 1) // 3, (n - 1) % 3, slots[(n - 1) % 2])
        if n > 0 and n % 3 == 0:
            stores[n // 3 - 1].start()
        if n > 3 and n % 3 == 1:
            gather(n // 3 - 1)
    gather(4)
    for r in range(32):
        for j in range(4):
            send_ref[4 * r + j] = sum_ref[16 * r : 16 * r + 16, 128 * j : 128 * j + 128].astype(BF)
    for copy in stores:
        copy.wait()


def coarse_kernel(
    taps_ref,
    last_ref,
    bias_ref,
    weight_ref,
    pairs_far,
    cells_far,
    owner_far,
    coarse_ref,
    feat_ref,
    wide_ref,
    tall_ref,
    first_ref,
    second_ref,
    third_ref,
    pairs_ref,
    cells_ref,
    owner_ref,
    arrive,
):
    fetch = [
        pltpu.make_async_copy(pairs_far.at[u], pairs_ref.at[u], arrive.at[u]) for u in range(5)
    ]
    fetch += [
        pltpu.make_async_copy(cells_far, cells_ref, arrive.at[5]),
        pltpu.make_async_copy(owner_far, owner_ref, arrive.at[6]),
    ]
    for copy in fetch:
        copy.start()

    edges = dot_nn(last_ref[...], taps_ref[...])
    edge = edges[:, 0:128]
    for n, shift in enumerate((127, 112, 111)):
        edge = edge + pltpu.roll(edges[:, 128 * n + 128 : 128 * n + 256], shift, 0)
    bias = bias_ref[...]
    bottom = iota((128, 128), 0) == 127
    slots = (first_ref, second_ref, third_ref)
    for u in range(5):
        fetch[u].wait()
        slots[u % 3][...] = dot_nn(pairs_ref[u].reshape(1152, 512), taps_ref[...])
        if u == 0:
            continue
        near, far = slots[(u - 1) % 3], slots[u % 3]
        for v in range(8):
            at = 128 * v
            total = (near[at : at + 128, 0:128] + near[at + 128 : at + 256, 128:256]) + (
                far[at : at + 128, 256:384] + far[at + 128 : at + 256, 384:512]
            )
            row = 16 * (u - 1) + v
            deep = jnp.where(bottom, edge[row : row + 1], pltpu.roll(total, 127, 0))
            value = total + pltpu.roll(deep, 64, 1) + bias
            at = 1024 * (u - 1) + 128 * v
            tall_ref[at : at + 128, :] = value.astype(BF)

    eye = ones_where(iota((64, 128), 0) == iota((64, 128), 1))
    wide_ref[...] = dot_nt(eye, tall_ref[...])
    fetch[5].wait()
    fetch[6].wait()
    picked = dot_nn(wide_ref[...].astype(BF), cells_ref[...]) * weight_ref[...]
    feat = jnp.zeros((1024, 128), F32)
    none = jnp.zeros((64, 256), BF)
    for part in split(picked):
        twice = jnp.concatenate(
            [jnp.concatenate([part, none], axis=1), jnp.concatenate([none, part], axis=1)], axis=0
        )
        feat = feat + dot_nt(owner_ref[...], twice)
    feat_ref[...] = feat.astype(BF).reshape(128, 8, 128)

    row, col = iota((256, 256), 0), iota((256, 256), 1)
    turn = ones_where(col == (row & 31) * 8 + (row >> 5))
    for g in range(8):
        tall = jnp.concatenate(
            [wide_ref[8 * g : 8 * g + 8, 128 * uv : 128 * uv + 128] for uv in range(32)], axis=0
        )
        part = dot_nn(turn, tall.astype(BF)).astype(BF)
        coarse_ref[8 * g : 8 * g + 8] = part.reshape(8, 32, 128)


def sum_kernel(scale, parts_ref, feat_ref, out_ref):
    total = jnp.sum(parts_ref[...].astype(F32), axis=0) * scale
    out_ref[:, 0:16, :] = jnp.broadcast_to(total.astype(BF)[None], (128, 16, 128))
    out_ref[:, 16:24, :] = feat_ref[...]


def finish_kernel(arrived_ref, grad_ref, feat_ref):
    eye = ones_where(iota((128, 128), 0) == iota((128, 128), 1))
    for a in range(2):
        for b in range(2):
            for d in range(2):
                base = 4 * (4 * a + 2 * b + d)
                for p in range(4):
                    block = jnp.concatenate(
                        [arrived_ref[4 * (base + t) + p, 0:16, :] for t in range(4)], axis=0
                    )
                    tap = ((2 * a + p // 2) * 4 + 2 * b + p % 2) * 4 + 2 * d
                    grad_ref[64 * tap : 64 * tap + 128, :] = dot_nt(eye, block)
    feat = jnp.sum(arrived_ref[:, 16:24, :].astype(F32), axis=0)
    feat_ref[0:8, :] = feat[:, 0:64]
    feat_ref[8:16, :] = pltpu.roll(feat, 64, 1)[:, 0:64]


VMEM, SMEM, HBM = pltpu.VMEM, pltpu.SMEM, pltpu.HBM


def call(kernel, outs, scratch=(), spaces=None, semaphores=(), cost=0, room=56):
    extra = {}
    if spaces is not None:
        places = [pl.BlockSpec(memory_space=space) for space in spaces]
        extra = {"in_specs": places[: -len(outs)], "out_specs": places[-len(outs) :]}
    return pl.pallas_call(
        kernel,
        out_shape=[jax.ShapeDtypeStruct(shape, dtype) for shape, dtype in outs],
        scratch_shapes=[pltpu.VMEM(shape, dtype) for shape, dtype in scratch]
        + [pltpu.SemaphoreType.DMA((count,)) for count in semaphores],
        compiler_params=pltpu.CompilerParams(vmem_limit_bytes=room << 20),
        cost_estimate=pl.CostEstimate(flops=cost, bytes_accessed=1 << 20, transcendentals=0),
        interpret=INTERPRET,
        **extra,
    )


def pack(fields, well_grad):
    outs = [((16, 8, 40, 128), BF)]
    return call(pack_kernel, outs, outs, [VMEM, VMEM, HBM], (4,), cost=1 << 31)(
        fields.reshape(16, 128, 128), well_grad
    )[0].reshape(128, 40, 128)


def prepare(perf_well, perf_cell, well_slot, w_lift, down_weight, field_grad):
    flat = jnp.pad(w_lift.reshape(216, 64), ((0, 40), (0, 0)))
    none = jnp.zeros_like(flat)
    lift = jnp.concatenate(
        [jnp.concatenate([flat, none], axis=1), jnp.concatenate([none, flat], axis=1)], axis=0
    )
    outs = [
        ((4096, 256), BF),
        ((256, 1024), BF),
        ((256, 512), BF),
        ((1024, 512), BF),
        ((512, 640), BF),
        ((512, 512), BF),
        ((512, 512), BF),
        ((64, 4096), BF),
    ]
    return call(prep_kernel, outs, cost=1 << 32)(
        perf_well,
        perf_cell,
        well_slot.reshape(1, 2048),
        lift,
        down_weight.reshape(4096, 64),
        field_grad.reshape(64, 32, 128),
    )


def lift(tile, arrived, perf_weight, b_lift, cells, rows, half, lanes, big, grad):
    outs = [((128, 16, 128), BF), ((128, 512), BF), ((5, 9, 128, 512), BF)]
    scratch = [
        ((1280, 512), BF),
        ((5, 1280, 128), BF),
        ((5, 1280, 128), BF),
        ((5, 16, 256), F32),
        ((384, 512), F32),
        ((384, 512), F32),
        ((128, 4096), BF),
        ((512, 512), F32),
        ((5, 9, 128, 512), BF),
        ((4096, 256), BF),
        ((256, 1024), BF),
        ((256, 512), BF),
        ((512, 512), BF),
        ((64, 4096), BF),
        ((128, 40, 128), BF),
        ((512, 640), BF),
    ]
    spaces = [SMEM] + [VMEM] * 2 + [HBM] * 7 + [VMEM, VMEM, HBM]
    bias = jnp.tile(0.5 * b_lift, 8)[None, :]
    return call(lift_kernel, outs, scratch, spaces, (8, 5), cost=1 << 33, room=ROOM_LIFT)(
        tile, perf_weight, bias, arrived, lanes, cells, rows, half, big, grad
    )


def coarsen(pairs, last, taps, b_down, perf_weight, cells, owner):
    outs = [((64, 32, 128), BF), ((128, 8, 128), BF)]
    scratch = [
        ((64, 4096), F32),
        ((4096, 128), BF),
        ((1152, 512), F32),
        ((1152, 512), F32),
        ((1152, 512), F32),
        ((5, 9, 128, 512), BF),
        ((4096, 256), BF),
        ((1024, 512), BF),
    ]
    spaces = [VMEM] * 4 + [HBM] * 3 + [VMEM] * 2
    bias = jnp.tile(b_down, 2)[None, :]
    return call(coarse_kernel, outs, scratch, spaces, (7,), cost=1 << 33)(
        taps, last, bias, perf_weight, pairs, cells, owner
    )


def finish(shared):
    outs = [((4096, 64), F32), ((16, 64), F32)]
    return call(finish_kernel, outs, cost=1 << 28, room=8)(shared)


def exchange(blocks):
    return lax.all_to_all(blocks, AXES, split_axis=0, concat_axis=0, tiled=True)


def body(
    fields,
    w_lift,
    b_lift,
    down_weight,
    b_down,
    perf_well,
    perf_cell,
    perf_weight,
    well_slot,
    well_grad,
    field_grad,
):
    scale = 1.0 / math.sqrt(64 * 64 * 128)
    tile = jnp.stack([lax.axis_index("gx"), lax.axis_index("gy")]).astype(I32)
    arrived = exchange(pack(fields, well_grad))
    cells, rows, half, owner, lanes, big, taps, grad = prepare(
        perf_well, perf_cell, well_slot, w_lift, down_weight, field_grad
    )
    parts, last, pairs = lift(
        tile, arrived, perf_weight, b_lift, cells, rows, half, lanes, big, grad
    )
    parts = exchange(parts)
    coarse, feat = coarsen(pairs, last, taps, b_down, perf_weight, cells, owner)
    shared = call(
        lambda *refs: sum_kernel(scale, *refs), [((128, 24, 128), BF)], cost=1 << 20, room=8
    )(parts, feat)[0]
    shared = exchange(shared)
    down_grad, well_feat = finish(shared)
    return (
        coarse.reshape(64, 4, 8, 128),
        well_feat,
        down_grad.reshape(4, 4, 4, 64, 64),
    )


def solution(mesh):
    placed = (
        P(None, AXES, None, None),
        P(),
        P(),
        P(),
        P(),
        P(AXES, None),
        P(AXES, None),
        P(AXES, None),
        P(),
        P(AXES, None),
        P(None, "gx", "gy", None),
    )
    return jax.shard_map(
        body,
        mesh=mesh,
        in_specs=placed,
        out_specs=(P(None, "gx", "gy", None), P(AXES, None), P()),
        check_vma=False,
    )
```
